768 devices in a mesh: slab: 24 (over z_lo, x), angle: 32 (over z_hi, y, core).
Axes of the slice: x: 4, y: 8, z: 12 (z_hi: 2, z_lo: 6; z = z_hi * 6 + z_lo), core: 2. Of those that a mesh axis runs over, the one named last changes fastest.
Arguments:
- volume: bfloat16 [192, 128, 2048], P('slab', 'angle'), may hold values from -6 to 6
- measured: float32 [32, 192, 2048], P('angle', 'slab'), may hold values from -6 to 6
- ray_tiles: bfloat16 [32, 128, 2, 128, 128], P(None, 'angle'), may hold values from -0.03125 to 0.03125
- tile_offsets: int32 [32, 128], replicated, may hold values from -3 to 3
- band_counts: int32 [32, 128], replicated, may hold values from 1 to 2
Outputs:
- updated: float32 [192, 128, 2048], P('slab', 'angle')
- residual: float32 [32, 192, 2048], P('angle', 'slab')
The draws below stay inside these ranges and needn't reach their ends.
All inputs are finite; a program needn't handle non-finite values.
Results may differ from the reference program's by a relative error of at most 0.00056.
Values may be sent and summed in bfloat16 or wider, within the bound.
No kernel may reach another device: no remote copies, remote signals or barrier semaphores. Data moves between devices by JAX's collectives and lax.ppermute only.
A program may use at most 64 MiB of HBM per device.

```python
import jax
import jax.numpy as jnp
from jax import lax

NX = 2048
TILE = 128
BAND = 2
OFFMAX = 3
NZ = 192
NY = 128
SUBSET = 32


def with_ends(array, own_key, smallest, high):
    longest = array.shape.index(max(array.shape))
    spots = []
    for shift in (0, 1):
        where = [jax.random.randint(jax.random.fold_in(own_key, axis), (), 0, length) for axis, length in enumerate(array.shape)]
        where[longest] = (where[longest] + shift) % array.shape[longest]
        spots.append(tuple(where))
    return array.at[spots[0]].set(smallest).at[spots[1]].set(high)


def steps_of(rng, extent, pieces, smallest, high):
    loudness = 1.0
    for dim, shards_of in pieces:
        steps = jax.random.uniform(jax.random.fold_in(jax.random.fold_in(rng, 6), dim), (shards_of,), jnp.float32, smallest / len(pieces), high / len(pieces))
        loudness = loudness * jnp.repeat(jnp.exp(steps), extent[dim] // shards_of).reshape((-1,) + (1,) * (len(extent) - 1 - dim))
    return loudness


def bell_draw(key, extent, scale, limit, pieces=(), kind=jnp.bfloat16):
    entries = jax.random.normal(key, extent, jnp.float32) * scale
    if len(pieces) > 0:
        entries = steps_of(key, extent, pieces, -0.22, 0.18) * entries
    return jnp.clip(entries, min=-limit, max=limit).astype(kind)


def setup_inputs(seed: int = 0) -> dict:
    keys = jax.random.split(jax.random.key(seed), 6)
    return {
        "volume": bell_draw(keys[0], (NZ, NY, NX), 1.0, 6.0, ((0, 24), (1, 32))),
        "measured": bell_draw(keys[1], (SUBSET, NZ, NX), 1.0, 6.0, ((0, 32), (1, 24)), jnp.float32),
        "ray_tiles": bell_draw(keys[2], (SUBSET, NY, BAND, TILE, TILE), (NY * BAND * TILE) ** -0.5, 0.03125, ((1, 32),)),
        "tile_offsets": with_ends(jax.random.randint(keys[3], (SUBSET, NY), 0 - OFFMAX, OFFMAX + 1), jax.random.fold_in(keys[3], 1), 0 - OFFMAX, OFFMAX).astype(jnp.int32),
        "band_counts": with_ends(jax.random.randint(keys[4], (SUBSET, NY), 1, BAND + 1), jax.random.fold_in(keys[4], 1), 1, BAND).astype(jnp.int32),
    }


step_size = 0.3
smooth_weight = 0.2
smooth_floor = 0.25

def shift_table(tile_offsets, band_counts, band):
    center = band // 2
    shifts = jnp.stack([tile_offsets + (k - center) for k in range(band)], axis=1).astype(jnp.int32)
    masks = jnp.stack([band_counts > k for k in range(band)], axis=1).astype(jnp.bfloat16)
    return (shifts, masks)

def project_angle(padded, shifts, masks, tiles, margin):
    tile_count = padded.shape[2] - 2 * margin
    summed = jnp.zeros((padded.shape[0], tile_count, padded.shape[3]), jnp.float32)
    for k in range(tiles.shape[1]):
        moved = jax.vmap(lambda block, offset: lax.dynamic_slice_in_dim(block, (margin + offset).astype(jnp.int32), tile_count, 1), in_axes=(1, 0), out_axes=1)(padded, shifts[k])
        moved = moved * masks[k][None, :, None, None]
        summed = summed + jnp.einsum('zrtc,rcd->ztd', moved.astype(jnp.float32), tiles[:, k].astype(jnp.float32))
    return summed.reshape(padded.shape[0], tile_count * padded.shape[3])

def spread_angle(view_pad, shifts, masks, tiles, margin):
    tile_count = view_pad.shape[1] - 2 * margin
    rows_here = shifts.shape[1]
    summed = jnp.zeros((view_pad.shape[0], rows_here, tile_count, view_pad.shape[2]), jnp.float32)
    for k in range(tiles.shape[1]):
        moved = jax.vmap(lambda offset: lax.dynamic_slice_in_dim(view_pad, (margin - offset).astype(jnp.int32), tile_count, 1), out_axes=1)(shifts[k])
        product = jnp.einsum('zrtd,rcd->zrtc', moved.astype(jnp.float32), tiles[:, k].astype(jnp.float32))
        summed = summed + product * masks[k].astype(jnp.float32)[None, :, None, None]
    return summed.reshape(view_pad.shape[0], rows_here, tile_count * view_pad.shape[2])

def divergence(field):
    base = field[:-1, :-1, :-1]
    step_z = field[1:, :-1, :-1] - base
    step_y = field[:-1, 1:, :-1] - base
    step_x = field[:-1, :-1, 1:] - base
    scale = jnp.sqrt(step_z * step_z + step_y * step_y + step_x * step_x + smooth_floor)
    flow_z = step_z / scale
    flow_y = step_y / scale
    flow_x = step_x / scale
    result = flow_z[1:, 1:, 1:] - flow_z[:-1, 1:, 1:]
    result = result + flow_y[1:, 1:, 1:] - flow_y[1:, :-1, 1:]
    return result + flow_x[1:, 1:, 1:] - flow_x[1:, 1:, :-1]

def reference(volume, measured, ray_tiles, tile_offsets, band_counts):
    depth, rows_all, width = volume.shape
    band = ray_tiles.shape[2]
    tile = ray_tiles.shape[3]
    margin = OFFMAX + band
    tile_count = width // tile
    shifts, masks = shift_table(tile_offsets, band_counts, band)
    blocks = volume.reshape(depth, rows_all, tile_count, tile)
    padded = jnp.pad(blocks, ((0, 0), (0, 0), (margin, margin), (0, 0)))

    def one_view(items):
        return project_angle(padded, items[0], items[1], items[2], margin)
    views = lax.map(one_view, (shifts, masks, ray_tiles))
    residual = views - measured
    rounded = residual.astype(jnp.bfloat16)
    view_blocks = rounded.reshape(rounded.shape[0], depth, tile_count, tile)
    view_pad = jnp.pad(view_blocks, ((0, 0), (0, 0), (margin, margin), (0, 0)))

    def accumulate(carry, items):
        return (carry + spread_angle(items[0], items[1], items[2], items[3], margin), None)
    gradient, unused = lax.scan(accumulate, jnp.zeros((depth, rows_all, width), jnp.float32), (view_pad, shifts, masks, ray_tiles))
    field = jnp.pad(volume.astype(jnp.float32), 1)
    updated = volume.astype(jnp.float32) - step_size * gradient + step_size * smooth_weight * divergence(field)
    return (updated, residual)
```

```python
from functools import partial

import jax
import jax.numpy as jnp
from jax import lax
from jax.experimental import pallas as pl
from jax.experimental.pallas import tpu as pltpu
from jax.sharding import Mesh, PartitionSpec as P

OFFMAX = 3

step_size = 0.3
smooth_weight = 0.2
smooth_floor = 0.25

ZHI, YS, CORES = 2, 8, 2
SLAB = ("zlo", "x")
ANGLE = ("zhi", "y", "core")

PAIR_SCALE = 2.0**6
PLANE_SCALE = 2.0**3


def padded_2(shard, sides, width):
    for axis, dim in sides:
        size, length = (lax.axis_size(axis), shard.shape[dim])
        up = [(i, (i + 1) % size) for i in range(size - 1)]
        down = [(j, i) for i, j in up]
        last = lax.slice_in_dim(shard, length - width, length, axis=dim)
        initial = lax.slice_in_dim(shard, 0, width, axis=dim)
        before = lax.ppermute(last, axis, up)
        after = lax.ppermute(initial, axis, down)
        shard = jnp.concatenate([before, shard, after], axis=dim)
    return shard


def divergence(field):
    base = field[:-1, :-1, :-1]
    step_z = field[1:, :-1, :-1] - base
    step_y = field[:-1, 1:, :-1] - base
    step_x = field[:-1, :-1, 1:] - base
    scale = jnp.sqrt(step_z * step_z + step_y * step_y + step_x * step_x + smooth_floor)
    flow_z = step_z / scale
    flow_y = step_y / scale
    flow_x = step_x / scale
    result = flow_z[1:, 1:, 1:] - flow_z[:-1, 1:, 1:]
    result = result + flow_y[1:, 1:, 1:] - flow_y[1:, :-1, 1:]
    return result + flow_x[1:, 1:, 1:] - flow_x[1:, 1:, :-1]


PAD = 4


def window_start(tile, copy_rows):
    return tile * 8 + (tile & 1) * (copy_rows - 8)


def band_windows(offset, count, sign, copy_rows):
    first = PAD + sign * (offset - 1)
    second = first + sign
    second_row = jnp.where(count > 1, window_start(second, copy_rows), 2 * copy_rows)
    return [pl.multiple_of(start, 16) for start in (window_start(first, copy_rows), second_row)]


def fill_windows(ref, index, block):
    rows = block.shape[0]
    wide = block.astype(jnp.float32)
    zero = lambda n: jnp.zeros((n, wide.shape[1]), jnp.float32)
    copy_rows = rows + 16 * PAD
    ref[index, :copy_rows] = jnp.concatenate([zero(8 * PAD), wide, zero(8 * PAD)], 0).astype(ref.dtype)
    ref[index, copy_rows : 2 * copy_rows] = jnp.concatenate(
        [zero(8 * (PAD - 1)), wide, zero(8 * (PAD + 1))], 0
    ).astype(ref.dtype)


def project_kernel(place, offsets, counts, volume, tiles, out, windows, *, scale):
    per_step = tiles.shape[1]
    rows, band = tiles.shape[3], tiles.shape[4]
    count = volume.shape[1]
    step = pl.program_id(0)

    @pl.when(step == 0)
    def _():
        for r in range(rows):
            fill_windows(windows, r, volume[r])
            windows[r, 2 * (count + 16 * PAD) :] = jnp.zeros((count, windows.shape[2]), windows.dtype)

    for i in range(per_step):
        for zh in range(ZHI):
            angle = (zh * YS + step * per_step + i) * CORES + place[0]
            pieces = []
            for r in range(rows):
                row = place[1] + r
                for start in band_windows(offsets[angle, row], counts[angle, row], 1, count + 16 * PAD):
                    pieces.append(windows[r, pl.ds(start, count), :])
            weights = tiles[zh, i, 0].reshape(rows * band * tiles.shape[5], tiles.shape[6])
            view = jnp.dot(jnp.concatenate(pieces, 1), weights, preferred_element_type=jnp.float32)
            out[i, zh] = (view * scale).astype(out.dtype)


def spread_kernel(place, offsets, counts, views, tiles, begin, out, windows):
    per_step = tiles.shape[1]
    rows = tiles.shape[3]
    count = views.shape[2]
    step = pl.program_id(0)

    @pl.when(step == 0)
    def _():
        for j in range(windows.shape[0]):
            windows[j, 2 * (count + 16 * PAD) :] = jnp.zeros((count, windows.shape[2]), windows.dtype)
        out[...] = begin[...]

    for i in range(per_step):
        for zh in range(ZHI):
            fill_windows(windows, i * ZHI + zh, views[i, zh])
    for r in range(rows):
        lhs, rhs = [], []
        for i in range(per_step):
            for zh in range(ZHI):
                angle = (zh * YS + step * per_step + i) * CORES + place[0]
                row = place[1] + r
                starts = band_windows(offsets[angle, row], counts[angle, row], -1, count + 16 * PAD)
                for k, start in enumerate(starts):
                    lhs.append(windows[i * ZHI + zh, pl.ds(start, count), :])
                    rhs.append(tiles[zh, i, 0, r, k])
        out[r] += lax.dot_general(
            jnp.concatenate(lhs, 1),
            jnp.concatenate(rhs, 1),
            (((1,), (1,)), ((), ())),
            preferred_element_type=jnp.float32,
        )


def tile_spec(tiles, per_step):
    return pl.BlockSpec(
        (ZHI, per_step, 1) + tiles.shape[3:], lambda i, place, offsets, counts: (0, i, place[0], 0, 0, 0, 0)
    )


def window_rows(count):
    return 3 * count + 32 * PAD


def project(place, offsets, counts, volume, tiles, dtype, scale, per_step=2):
    rows, count, lanes = volume.shape
    flops = 2 * ZHI * YS * count * lanes * tiles.shape[3] * tiles.shape[4] * lanes
    return pl.pallas_call(
        partial(project_kernel, scale=scale),
        grid_spec=pltpu.PrefetchScalarGridSpec(
            num_scalar_prefetch=3,
            grid=(YS // per_step,),
            in_specs=[
                pl.BlockSpec(volume.shape, lambda i, place, offsets, counts: (0, 0, 0)),
                tile_spec(tiles, per_step),
            ],
            out_specs=pl.BlockSpec((per_step, ZHI, count, lanes), lambda i, place, offsets, counts: (i, 0, 0, 0)),
            scratch_shapes=[pltpu.VMEM((rows, window_rows(count), lanes), jnp.bfloat16)],
        ),
        out_shape=jax.ShapeDtypeStruct((YS, ZHI, count, lanes), dtype),
        compiler_params=pltpu.CompilerParams(
            dimension_semantics=("arbitrary",), vmem_limit_bytes=16 << 20
        ),
        cost_estimate=pl.CostEstimate(flops=flops, bytes_accessed=tiles.size, transcendentals=0),
        name="project",
    )(place, offsets, counts, volume, tiles)


def spread(place, offsets, counts, views, tiles, begin, per_step=2):
    rows, count, lanes = begin.shape
    flops = 2 * ZHI * YS * count * lanes * tiles.shape[3] * tiles.shape[4] * lanes
    return pl.pallas_call(
        spread_kernel,
        grid_spec=pltpu.PrefetchScalarGridSpec(
            num_scalar_prefetch=3,
            grid=(YS // per_step,),
            in_specs=[
                pl.BlockSpec((per_step, ZHI, count, lanes), lambda i, place, offsets, counts: (i, 0, 0, 0)),
                tile_spec(tiles, per_step),
                pl.BlockSpec(begin.shape, lambda i, place, offsets, counts: (0, 0, 0)),
            ],
            out_specs=pl.BlockSpec(begin.shape, lambda i, place, offsets, counts: (0, 0, 0)),
            scratch_shapes=[pltpu.VMEM((per_step * ZHI, window_rows(count), lanes), jnp.bfloat16)],
        ),
        out_shape=jax.ShapeDtypeStruct(begin.shape, jnp.float32),
        compiler_params=pltpu.CompilerParams(
            dimension_semantics=("arbitrary",), vmem_limit_bytes=16 << 20
        ),
        cost_estimate=pl.CostEstimate(flops=flops, bytes_accessed=tiles.size, transcendentals=0),
        name="spread",
    )(place, offsets, counts, views, tiles, begin)


def swap(array, axis):
    return lax.ppermute(array, axis, [(0, 1), (1, 0)])


def per_device(volume, measured, ray_tiles, tile_offsets, band_counts):
    f32, f16, bf16 = jnp.float32, jnp.float16, jnp.bfloat16
    depth, row_count, width = volume.shape
    tile = ray_tiles.shape[3]
    tile_count = width // tile
    count = tile_count * depth
    zhi, core = lax.axis_index("zhi"), lax.axis_index("core")
    first_row = lax.axis_index(ANGLE) * row_count
    mine = jnp.stack([core, first_row])
    other = jnp.stack([1 - core, first_row])
    tiles = pltpu.with_memory_space_constraint(
        ray_tiles.reshape((ZHI, YS, CORES) + ray_tiles.shape[1:]), pltpu.HBM
    )
    by_row = (
        volume.reshape(depth, row_count, tile_count, tile).transpose(1, 2, 0, 3).reshape(row_count, count, tile)
    )

    away = project(other, tile_offsets, band_counts, by_row, tiles, f32, PAIR_SCALE)
    arrived = swap(away, "core")
    kept = project(mine, tile_offsets, band_counts, by_row, tiles, f32, PAIR_SCALE)
    pair = (kept + arrived).astype(f16)
    parts = lax.all_to_all(pair, "y", 0, 0, tiled=True)
    plane = jnp.sum(parts.astype(f32), axis=0) * (1 / PAIR_SCALE)
    seen = measured.reshape(depth, tile_count, tile).transpose(1, 0, 2).reshape(count, tile)
    is_mine = (lax.broadcasted_iota(jnp.int32, (ZHI, 1, 1), 0) == zhi)
    plane = plane - jnp.where(is_mine, seen[None], 0.0)
    far = swap((plane * PLANE_SCALE).astype(f16), "zhi")
    both = plane + far.astype(f32) * (1 / PLANE_SCALE)
    residual = jnp.where(zhi == 0, both[0], both[1])
    residual = residual.reshape(tile_count, depth, tile).transpose(1, 0, 2).reshape(1, depth, width)
    rounded = both.astype(bf16)
    views = lax.all_to_all(
        jnp.broadcast_to(rounded[None], (YS,) + rounded.shape), "y", 0, 0, tiled=True
    )
    views_other = swap(views, "core")
    gradient = spread(mine, tile_offsets, band_counts, views, tiles, jnp.zeros((row_count, count, tile), f32))
    gradient = spread(other, tile_offsets, band_counts, views_other, tiles, gradient)
    gradient = (
        gradient.reshape(row_count, tile_count, depth, tile).transpose(2, 0, 1, 3).reshape(depth, row_count, width)
    )

    beside_all = padded_2(volume, ((SLAB, 0), (ANGLE, 1)), 1)
    field = jnp.pad(beside_all.astype(f32), ((0, 0), (0, 0), (1, 1)))
    updated = volume.astype(f32) - step_size * gradient + step_size * smooth_weight * divergence(field)
    return (updated, residual)


def solution(mesh):
    slabs = mesh.shape["slab"]
    fine = Mesh(
        mesh.devices.reshape(slabs // 4, 4, ZHI, YS, CORES), SLAB + ANGLE
    )
    return jax.shard_map(
        per_device,
        mesh=fine,
        in_specs=(
            P(SLAB, ANGLE, None),
            P(ANGLE, SLAB, None),
            P(None, ANGLE, None, None, None),
            P(),
            P(),
        ),
        out_specs=(P(SLAB, ANGLE, None), P(ANGLE, SLAB, None)),
        check_vma=False,
    )
```

```python
from functools import partial

import jax
import jax.numpy as jnp
from jax import lax
from jax.experimental import pallas as pl
from jax.experimental.pallas import tpu as pltpu
from jax.sharding import Mesh, PartitionSpec as P

OFFMAX = 3

step_size = 0.3
smooth_weight = 0.2
smooth_floor = 0.25

ZHI, YS, CORES = 2, 8, 2
SLAB = ("zlo", "x")
ANGLE = ("zhi", "y", "core")

PAIR_SCALE = 2.0**6
PLANE_SCALE = 2.0**3


def shifts_of(size, gap=None):
    up = [(i, i + 1) for i in range(size - 1) if i != gap]
    return up, [(j, i) for i, j in up]


def edges(shard, dim):
    length = shard.shape[dim]
    return lax.slice_in_dim(shard, length - 1, length, axis=dim), lax.slice_in_dim(shard, 0, 1, axis=dim)


def with_row_neighbours(shard, ends_plane, begins_plane):
    size = lax.axis_size(ANGLE)
    gap = size // ZHI - 1
    up, down = shifts_of(size, gap)
    last, first = edges(shard, 1)
    before, after = lax.ppermute(last, ANGLE, up), lax.ppermute(first, ANGLE, down)
    across = lax.ppermute(jnp.where(ends_plane, last, first), ANGLE, [(gap, gap + 1), (gap + 1, gap)])
    before = jnp.where(begins_plane, across, before)
    after = jnp.where(ends_plane, across, after)
    return jnp.concatenate([before, shard, after], axis=1)


def with_slab_neighbours(shard):
    up, down = shifts_of(lax.axis_size(SLAB))
    last, first = edges(shard, 0)
    return jnp.concatenate([lax.ppermute(last, SLAB, up), shard, lax.ppermute(first, SLAB, down)], axis=0)


def divergence(field):
    base = field[:-1, :-1, :-1]
    step_z = field[1:, :-1, :-1] - base
    step_y = field[:-1, 1:, :-1] - base
    step_x = field[:-1, :-1, 1:] - base
    scale = jnp.sqrt(step_z * step_z + step_y * step_y + step_x * step_x + smooth_floor)
    flow_z = step_z / scale
    flow_y = step_y / scale
    flow_x = step_x / scale
    result = flow_z[1:, 1:, 1:] - flow_z[:-1, 1:, 1:]
    result = result + flow_y[1:, 1:, 1:] - flow_y[1:, :-1, 1:]
    return result + flow_x[1:, 1:, 1:] - flow_x[1:, 1:, :-1]


PAD = 4
GROUP = 4


def copy_rows(count):
    return count + 16 * PAD


def window_rows(bands, count):
    return bands * 2 * copy_rows(count) + count


def band_windows(offset, used, sign, band, bands, count):
    base = band * 2 * copy_rows(count)

    def start(tile):
        return base + tile * 8 + (tile & 1) * (copy_rows(count) - 8)

    first = PAD + sign * (offset - 1)
    second = jnp.where(used > 1, start(first + sign), bands * 2 * copy_rows(count))
    return pl.multiple_of(start(first), 16), pl.multiple_of(second, 16)


def fill_windows(ref, band, wide):
    count, lanes = wide.shape
    rows = copy_rows(count)
    zero = lambda n: jnp.zeros((n, lanes), wide.dtype)
    base = band * 2 * rows
    ref[base : base + rows] = jnp.concatenate([zero(8 * PAD), wide, zero(8 * PAD)], 0).astype(ref.dtype)
    ref[base + rows : base + 2 * rows] = jnp.concatenate(
        [zero(8 * (PAD - 1)), wide, zero(8 * (PAD + 1))], 0
    ).astype(ref.dtype)


def fill_zeros(ref, bands, count):
    base = bands * 2 * copy_rows(count)
    ref[base : base + count] = jnp.zeros((count, ref.shape[1]), ref.dtype)


def angle_of(j, core):
    return ((j % ZHI) * YS + j // ZHI) * CORES + core


def project_one(j, core, first_row, offsets, counts, windows, tiles, out, scale):
    rows = tiles.shape[1]
    count, lanes = out.shape[2:]
    angle = angle_of(j, core)
    pieces = []
    for r in range(rows):
        row = first_row + r
        for start in band_windows(offsets[angle, row], counts[angle, row], 1, r, rows, count):
            pieces.append(windows[pl.ds(start, count), :])
    weights = tiles[angle].reshape(len(pieces) * lanes, lanes)
    view = jnp.dot(jnp.concatenate(pieces, 1), weights, preferred_element_type=jnp.float32)
    out[j // ZHI, j % ZHI] = view * scale


def load_project_kernel(
    place, offsets_hbm, counts_hbm, volume_hbm, tiles_hbm, out, tiles, windows, offsets, counts, volume, tile_sems, sems,
    *, scale
):
    core, first_row = place[0], place[1]
    blocks, rows = ZHI * YS, tiles.shape[1]
    count, lanes = out.shape[2:]
    small = [
        pltpu.make_async_copy(source, target, sems.at[i])
        for i, (source, target) in enumerate(
            ((volume_hbm, volume), (offsets_hbm, offsets), (counts_hbm, counts))
        )
    ]
    copies = tile_copies(tiles_hbm, tiles, tile_sems, 1 - core)
    for copy in small + copies[:blocks]:
        copy.start()
    small[0].wait()
    for r in range(rows):
        line = volume[:, r, :].astype(jnp.float32)
        fill_windows(
            windows, r, jnp.concatenate([line[:, t * lanes : (t + 1) * lanes] for t in range(line.shape[1] // lanes)], 0)
        )
    fill_zeros(windows, rows, count)
    small[1].wait()
    small[2].wait()
    for first in range(0, blocks, GROUP):
        wait_group(copies, first)
        for j in range(first, first + GROUP):
            project_one(j, 1 - core, first_row, offsets, counts, windows, tiles, out, scale)
    for copy in copies[blocks:]:
        copy.wait()


def project_kernel(place, offsets, counts, windows, tiles, out, *, scale):
    for j in range(ZHI * YS):
        project_one(j, place[0], place[1], offsets, counts, windows, tiles, out, scale)


def tile_copies(tiles_hbm, tiles, sems, first_core):
    blocks = ZHI * YS
    order = [angle_of(j, first_core) for j in range(blocks)] + [angle_of(j, 1 - first_core) for j in range(blocks)]
    return [pltpu.make_async_copy(tiles_hbm.at[a], tiles.at[a], sems.at[i]) for i, a in enumerate(order)]


def wait_group(copies, first):
    blocks = ZHI * YS
    for copy in copies[first : first + GROUP]:
        copy.wait()
    if first == 0:
        for copy in copies[blocks:]:
            copy.start()


def spread_group(first, core, first_row, offsets, counts, windows, tiles, begin, out):
    blocks, rows = ZHI * YS, tiles.shape[1]
    count = out.shape[1]
    for r in range(rows):
        row = first_row + r
        lhs, rhs = [], []
        for j in range(first, first + GROUP):
            angle = angle_of(j, core)
            starts = band_windows(offsets[angle, row], counts[angle, row], -1, j, blocks, count)
            for k, start in enumerate(starts):
                lhs.append(windows[pl.ds(start, count), :])
                rhs.append(tiles[angle, r, k])
        part = lax.dot_general(
            jnp.concatenate(lhs, 1),
            jnp.concatenate(rhs, 1),
            (((1,), (1,)), ((), ())),
            preferred_element_type=jnp.float32,
        )
        if first > 0:
            out[r] += part
        elif begin is None:
            out[r] = part
        else:
            out[r] = begin[r] + part


def fill_views(windows, views):
    blocks = ZHI * YS
    for j in range(blocks):
        fill_windows(windows, j, views[j // ZHI, j % ZHI].astype(jnp.float32))
    fill_zeros(windows, blocks, views.shape[2])


def load_spread_kernel(place, offsets, counts, views, tiles_hbm, out, tiles, windows, sems):
    copies = tile_copies(tiles_hbm, tiles, sems, place[0])
    for copy in copies[: ZHI * YS]:
        copy.start()
    fill_views(windows, views)
    for first in range(0, ZHI * YS, GROUP):
        wait_group(copies, first)
        spread_group(first, place[0], place[1], offsets, counts, windows, tiles, None, out)
    for copy in copies[ZHI * YS :]:
        copy.wait()


def spread_kernel(place, offsets, counts, views, tiles, begin, out, windows):
    fill_views(windows, views)
    for first in range(0, ZHI * YS, GROUP):
        spread_group(first, 1 - place[0], place[1], offsets, counts, windows, tiles, begin, out)


ANY = pl.BlockSpec(memory_space=pl.ANY)
VMEM = pl.BlockSpec(memory_space=pltpu.VMEM)
SMEM = pl.BlockSpec(memory_space=pltpu.SMEM)


def params():
    return pltpu.CompilerParams(vmem_limit_bytes=16 << 20)


def cost(tiles, share):
    return pl.CostEstimate(
        flops=256 * tiles.size // share, bytes_accessed=2 * tiles.size // share, transcendentals=0
    )


def in_hbm(array):
    return pltpu.with_memory_space_constraint(array, pltpu.HBM)


def load_project(place, offsets, counts, volume, tiles, scale):
    depth, rows, width = volume.shape
    lanes = tiles.shape[-1]
    count = depth * width // lanes
    return pl.pallas_call(
        partial(load_project_kernel, scale=scale),
        in_specs=[SMEM, ANY, ANY, ANY, ANY],
        out_specs=[VMEM, VMEM, VMEM, SMEM, SMEM],
        out_shape=[
            pltpu.VMEM((YS, ZHI, count, lanes), jnp.float32),
            pltpu.VMEM(tiles.shape, tiles.dtype),
            pltpu.VMEM((window_rows(rows, count), lanes), volume.dtype),
            pltpu.SMEM(offsets.shape, offsets.dtype),
            pltpu.SMEM(counts.shape, counts.dtype),
        ],
        scratch_shapes=[
            pltpu.VMEM(volume.shape, volume.dtype),
            pltpu.SemaphoreType.DMA((tiles.shape[0],)),
            pltpu.SemaphoreType.DMA((3,)),
        ],
        compiler_params=params(),
        cost_estimate=cost(tiles, 2),
        name="load_project",
    )(place, in_hbm(offsets), in_hbm(counts), in_hbm(volume), in_hbm(tiles))


def project(place, offsets, counts, windows, tiles, like, scale):
    return pl.pallas_call(
        partial(project_kernel, scale=scale),
        in_specs=[SMEM, SMEM, SMEM, VMEM, VMEM],
        out_specs=VMEM,
        out_shape=pltpu.VMEM(like.shape, jnp.float32),
        compiler_params=params(),
        cost_estimate=cost(tiles, 2),
        name="project",
    )(place, offsets, counts, windows, tiles)


def load_spread(place, offsets, counts, views, tiles):
    count, lanes = views.shape[2:]
    return pl.pallas_call(
        load_spread_kernel,
        in_specs=[SMEM, SMEM, SMEM, VMEM, ANY],
        out_specs=[VMEM, VMEM],
        out_shape=[
            pltpu.VMEM((tiles.shape[1], count, lanes), jnp.float32),
            pltpu.VMEM(tiles.shape, tiles.dtype),
        ],
        scratch_shapes=[
            pltpu.VMEM((window_rows(ZHI * YS, count), lanes), jnp.bfloat16),
            pltpu.SemaphoreType.DMA((tiles.shape[0],)),
        ],
        compiler_params=params(),
        cost_estimate=cost(tiles, 2),
        name="load_spread",
    )(place, offsets, counts, views, in_hbm(tiles))


def spread(place, offsets, counts, views, tiles, begin):
    count, lanes = views.shape[2:]
    return pl.pallas_call(
        spread_kernel,
        in_specs=[SMEM, SMEM, SMEM, VMEM, VMEM, VMEM],
        out_specs=VMEM,
        out_shape=pltpu.VMEM((tiles.shape[1], count, lanes), jnp.float32),
        scratch_shapes=[pltpu.VMEM((window_rows(ZHI * YS, count), lanes), jnp.bfloat16)],
        compiler_params=params(),
        cost_estimate=cost(tiles, 2),
        name="spread",
    )(place, offsets, counts, views, tiles, begin)


def swap(array, axis):
    return lax.ppermute(array, axis, [(0, 1), (1, 0)])


def per_device(volume, measured, ray_tiles, tile_offsets, band_counts):
    f32, f16, bf16 = jnp.float32, jnp.float16, jnp.bfloat16
    depth, row_count, width = volume.shape
    tile = ray_tiles.shape[3]
    tile_count = width // tile
    count = tile_count * depth
    zhi, core = lax.axis_index("zhi"), lax.axis_index("core")
    me = lax.axis_index(ANGLE)
    first_row = me * row_count
    gap = lax.axis_size(ANGLE) // ZHI - 1
    is_mine = lax.broadcasted_iota(jnp.int32, (ZHI, 1, 1), 0) == zhi
    place, is_mine, low_plane, ends_plane, begins_plane = lax.optimization_barrier(
        (jnp.stack([core, first_row]), is_mine, zhi == 0, me == gap, me == gap + 1)
    )

    away, tiles, windows, offsets, counts = load_project(
        place, tile_offsets, band_counts, volume, ray_tiles, PAIR_SCALE
    )
    arrived = swap(away, "core")
    kept = project(place, offsets, counts, windows, tiles, away, PAIR_SCALE)
    pair = (kept + arrived).astype(f16)
    parts = lax.all_to_all(pair, "y", 0, 0, tiled=True)
    plane = jnp.sum(parts.astype(f32), axis=0) * (1 / PAIR_SCALE)
    seen = measured.reshape(depth, tile_count, tile).transpose(1, 0, 2).reshape(count, tile)
    plane = plane - jnp.where(is_mine, seen[None], 0.0)
    far = swap((plane * PLANE_SCALE).astype(f16), "zhi")
    both = plane + far.astype(f32) * (1 / PLANE_SCALE)
    residual = jnp.where(low_plane, both[0], both[1])
    residual = residual.reshape(tile_count, depth, tile).transpose(1, 0, 2).reshape(1, depth, width)
    rounded = both.astype(bf16)
    views = lax.all_to_all(
        jnp.broadcast_to(rounded[None], (YS,) + rounded.shape), "y", 0, 0, tiled=True
    )
    views_other = swap(views, "core")
    gradient, tiles = load_spread(place, offsets, counts, views, ray_tiles)
    gradient = spread(place, offsets, counts, views_other, tiles, gradient)
    gradient = (
        gradient.reshape(row_count, tile_count, depth, tile).transpose(2, 0, 1, 3).reshape(depth, row_count, width)
    )

    beside_all = with_slab_neighbours(with_row_neighbours(volume, ends_plane, begins_plane))
    field = jnp.pad(beside_all.astype(f32), ((0, 0), (0, 0), (1, 1)))
    updated = volume.astype(f32) - step_size * gradient + step_size * smooth_weight * divergence(field)
    return (updated, residual)


def solution(mesh):
    slabs = mesh.shape["slab"]
    fine = Mesh(
        mesh.devices.reshape(slabs // 4, 4, ZHI, YS, CORES), SLAB + ANGLE
    )
    return jax.shard_map(
        per_device,
        mesh=fine,
        in_specs=(
            P(SLAB, ANGLE, None),
            P(ANGLE, SLAB, None),
            P(None, ANGLE, None, None, None),
            P(),
            P(),
        ),
        out_specs=(P(SLAB, ANGLE, None), P(ANGLE, SLAB, None)),
        check_vma=False,
    )
```

```python
from functools import partial

import jax
import jax.numpy as jnp
from jax import lax
from jax.experimental import pallas as pl
from jax.experimental.pallas import tpu as pltpu
from jax.sharding import Mesh, PartitionSpec as P

OFFMAX = 3

step_size = 0.3
smooth_weight = 0.2
smooth_floor = 0.25

ZHI, YS, CORES = 2, 8, 2
SLAB = ("zlo", "x")
ANGLE = ("zhi", "y", "core")

PAIR_SCALE = 2.0**6
PLANE_SCALE = 2.0**3


def shifts_of(size, gap=None):
    up = [(i, i + 1) for i in range(size - 1) if i != gap]
    return up, [(j, i) for i, j in up]


def edges(shard, dim):
    length = shard.shape[dim]
    return lax.slice_in_dim(shard, length - 1, length, axis=dim), lax.slice_in_dim(shard, 0, 1, axis=dim)


def with_row_neighbours(shard, ends_plane, begins_plane):
    size = lax.axis_size(ANGLE)
    gap = size // ZHI - 1
    up, down = shifts_of(size, gap)
    last, first = edges(shard, 1)
    before, after = lax.ppermute(last, ANGLE, up), lax.ppermute(first, ANGLE, down)
    across = lax.ppermute(jnp.where(ends_plane, last, first), ANGLE, [(gap, gap + 1), (gap + 1, gap)])
    before = jnp.where(begins_plane, across, before)
    after = jnp.where(ends_plane, across, after)
    return jnp.concatenate([before, shard, after], axis=1)


def with_slab_neighbours(shard):
    up, down = shifts_of(lax.axis_size(SLAB))
    last, first = edges(shard, 0)
    return jnp.concatenate([lax.ppermute(last, SLAB, up), shard, lax.ppermute(first, SLAB, down)], axis=0)


def divergence(field):
    base = field[:-1, :-1, :-1]
    step_z = field[1:, :-1, :-1] - base
    step_y = field[:-1, 1:, :-1] - base
    step_x = field[:-1, :-1, 1:] - base
    scale = jnp.sqrt(step_z * step_z + step_y * step_y + step_x * step_x + smooth_floor)
    flow_z = step_z / scale
    flow_y = step_y / scale
    flow_x = step_x / scale
    result = flow_z[1:, 1:, 1:] - flow_z[:-1, 1:, 1:]
    result = result + flow_y[1:, 1:, 1:] - flow_y[1:, :-1, 1:]
    return result + flow_x[1:, 1:, 1:] - flow_x[1:, 1:, :-1]


PAD = 4
GROUP = 4


def copy_rows(count):
    return count + 16 * PAD


def window_rows(bands, count):
    return bands * 2 * copy_rows(count) + count


def band_windows(offset, used, sign, band, bands, count):
    base = band * 2 * copy_rows(count)

    def start(tile):
        return base + tile * 8 + (tile & 1) * (copy_rows(count) - 8)

    first = PAD + sign * (offset - 1)
    second = jnp.where(used > 1, start(first + sign), bands * 2 * copy_rows(count))
    return pl.multiple_of(start(first), 16), pl.multiple_of(second, 16)


def fill_windows(ref, band, wide):
    count, lanes = wide.shape
    rows = copy_rows(count)
    zero = lambda n: jnp.zeros((n, lanes), wide.dtype)
    base = band * 2 * rows
    ref[base : base + rows] = jnp.concatenate([zero(8 * PAD), wide, zero(8 * PAD)], 0).astype(ref.dtype)
    ref[base + rows : base + 2 * rows] = jnp.concatenate(
        [zero(8 * (PAD - 1)), wide, zero(8 * (PAD + 1))], 0
    ).astype(ref.dtype)


def fill_zeros(ref, bands, count):
    base = bands * 2 * copy_rows(count)
    ref[base : base + count] = jnp.zeros((count, ref.shape[1]), ref.dtype)


def angle_of(j, core):
    return ((j % ZHI) * YS + j // ZHI) * CORES + core


def project_one(j, core, first_row, offsets, counts, windows, tiles, out, scale):
    rows = tiles.shape[1]
    count, lanes = out.shape[2:]
    angle = angle_of(j, core)
    pieces = []
    for r in range(rows):
        row = first_row + r
        for start in band_windows(offsets[angle, row], counts[angle, row], 1, r, rows, count):
            pieces.append(windows[pl.ds(start, count), :])
    weights = tiles[angle].reshape(len(pieces) * lanes, lanes)
    view = jnp.dot(jnp.concatenate(pieces, 1), weights, preferred_element_type=jnp.float32)
    out[j // ZHI, j % ZHI] = view * scale


def load_project_kernel(
    place, offsets_hbm, counts_hbm, volume_hbm, tiles_hbm, out, tiles, windows, offsets, counts, volume, tile_sems, sems,
    *, scale
):
    core, first_row = place[0], place[1]
    blocks, rows = ZHI * YS, tiles.shape[1]
    count, lanes = out.shape[2:]
    small = [
        pltpu.make_async_copy(source, target, sems.at[i])
        for i, (source, target) in enumerate(
            ((volume_hbm, volume), (offsets_hbm, offsets), (counts_hbm, counts))
        )
    ]
    copies = tile_copies(tiles_hbm, tiles, tile_sems, 1 - core)
    for copy in small + copies[:blocks]:
        copy.start()
    small[0].wait()
    for r in range(rows):
        line = volume[:, r, :].astype(jnp.float32)
        fill_windows(
            windows, r, jnp.concatenate([line[:, t * lanes : (t + 1) * lanes] for t in range(line.shape[1] // lanes)], 0)
        )
    fill_zeros(windows, rows, count)
    small[1].wait()
    small[2].wait()
    for first in range(0, blocks, GROUP):
        wait_group(copies, first)
        for j in range(first, first + GROUP):
            project_one(j, 1 - core, first_row, offsets, counts, windows, tiles, out, scale)
    for copy in copies[blocks:]:
        copy.wait()


def project_kernel(place, offsets, counts, windows, tiles, out, *, scale):
    for j in range(ZHI * YS):
        project_one(j, place[0], place[1], offsets, counts, windows, tiles, out, scale)


def tile_copies(tiles_hbm, tiles, sems, first_core):
    blocks = ZHI * YS
    order = [angle_of(j, first_core) for j in range(blocks)] + [angle_of(j, 1 - first_core) for j in range(blocks)]
    return [pltpu.make_async_copy(tiles_hbm.at[a], tiles.at[a], sems.at[i]) for i, a in enumerate(order)]


def wait_group(copies, first):
    blocks = ZHI * YS
    for copy in copies[first : first + GROUP]:
        copy.wait()
    if first == 0:
        for copy in copies[blocks:]:
            copy.start()


def spread_group(first, core, first_row, offsets, counts, windows, tiles, begin, out):
    blocks, rows = ZHI * YS, tiles.shape[1]
    count = out.shape[1]
    for r in range(rows):
        row = first_row + r
        lhs, rhs = [], []
        for j in range(first, first + GROUP):
            angle = angle_of(j, core)
            starts = band_windows(offsets[angle, row], counts[angle, row], -1, j, blocks, count)
            for k, start in enumerate(starts):
                lhs.append(windows[pl.ds(start, count), :])
                rhs.append(tiles[angle, r, k])
        part = lax.dot_general(
            jnp.concatenate(lhs, 1),
            jnp.concatenate(rhs, 1),
            (((1,), (1,)), ((), ())),
            preferred_element_type=jnp.float32,
        )
        if first > 0:
            out[r] += part
        elif begin is None:
            out[r] = part
        else:
            out[r] = begin[r] + part


def fill_views(windows, views):
    blocks = ZHI * YS
    for j in range(blocks):
        fill_windows(windows, j, views[j // ZHI, j % ZHI].astype(jnp.float32))
    fill_zeros(windows, blocks, views.shape[2])


def load_spread_kernel(place, offsets, counts, views, tiles_hbm, out, tiles, windows, sems):
    copies = tile_copies(tiles_hbm, tiles, sems, place[0])
    for copy in copies[: ZHI * YS]:
        copy.start()
    fill_views(windows, views)
    for first in range(0, ZHI * YS, GROUP):
        wait_group(copies, first)
        spread_group(first, place[0], place[1], offsets, counts, windows, tiles, None, out)
    for copy in copies[ZHI * YS :]:
        copy.wait()


def spread_kernel(place, offsets, counts, views, tiles, begin, base, out, total, windows):
    fill_views(windows, views)
    for first in range(0, ZHI * YS, GROUP):
        spread_group(first, 1 - place[0], place[1], offsets, counts, windows, tiles, begin, total)
    depth, rows, width = out.shape
    lanes = total.shape[2]
    for r in range(rows):
        for t in range(width // lanes):
            here = slice(t * lanes, (t + 1) * lanes)
            out[:, r, here] = base[:, r, here] - step_size * total[r, t * depth : (t + 1) * depth, :]


ANY = pl.BlockSpec(memory_space=pl.ANY)
VMEM = pl.BlockSpec(memory_space=pltpu.VMEM)
SMEM = pl.BlockSpec(memory_space=pltpu.SMEM)


def params():
    return pltpu.CompilerParams(vmem_limit_bytes=16 << 20)


def cost(tiles, share):
    return pl.CostEstimate(
        flops=256 * tiles.size // share, bytes_accessed=2 * tiles.size // share, transcendentals=0
    )


def in_hbm(array):
    return pltpu.with_memory_space_constraint(array, pltpu.HBM)


def load_project(place, offsets, counts, volume, tiles, scale):
    depth, rows, width = volume.shape
    lanes = tiles.shape[-1]
    count = depth * width // lanes
    return pl.pallas_call(
        partial(load_project_kernel, scale=scale),
        in_specs=[SMEM, ANY, ANY, ANY, ANY],
        out_specs=[VMEM, VMEM, VMEM, SMEM, SMEM],
        out_shape=[
            pltpu.VMEM((YS, ZHI, count, lanes), jnp.float32),
            pltpu.VMEM(tiles.shape, tiles.dtype),
            pltpu.VMEM((window_rows(rows, count), lanes), volume.dtype),
            pltpu.SMEM(offsets.shape, offsets.dtype),
            pltpu.SMEM(counts.shape, counts.dtype),
        ],
        scratch_shapes=[
            pltpu.VMEM(volume.shape, volume.dtype),
            pltpu.SemaphoreType.DMA((tiles.shape[0],)),
            pltpu.SemaphoreType.DMA((3,)),
        ],
        compiler_params=params(),
        cost_estimate=cost(tiles, 2),
        name="load_project",
    )(place, in_hbm(offsets), in_hbm(counts), in_hbm(volume), in_hbm(tiles))


def project(place, offsets, counts, windows, tiles, like, scale):
    return pl.pallas_call(
        partial(project_kernel, scale=scale),
        in_specs=[SMEM, SMEM, SMEM, VMEM, VMEM],
        out_specs=VMEM,
        out_shape=pltpu.VMEM(like.shape, jnp.float32),
        compiler_params=params(),
        cost_estimate=cost(tiles, 2),
        name="project",
    )(place, offsets, counts, windows, tiles)


def load_spread(place, offsets, counts, views, tiles):
    count, lanes = views.shape[2:]
    return pl.pallas_call(
        load_spread_kernel,
        in_specs=[SMEM, SMEM, SMEM, VMEM, ANY],
        out_specs=[VMEM, VMEM],
        out_shape=[
            pltpu.VMEM((tiles.shape[1], count, lanes), jnp.float32),
            pltpu.VMEM(tiles.shape, tiles.dtype),
        ],
        scratch_shapes=[
            pltpu.VMEM((window_rows(ZHI * YS, count), lanes), jnp.bfloat16),
            pltpu.SemaphoreType.DMA((tiles.shape[0],)),
        ],
        compiler_params=params(),
        cost_estimate=cost(tiles, 2),
        name="load_spread",
    )(place, offsets, counts, views, in_hbm(tiles))


def spread(place, offsets, counts, views, tiles, begin, base):
    count, lanes = views.shape[2:]
    return pl.pallas_call(
        spread_kernel,
        in_specs=[SMEM, SMEM, SMEM] + [VMEM] * 4,
        out_specs=VMEM,
        out_shape=jax.ShapeDtypeStruct(base.shape, base.dtype),
        scratch_shapes=[
            pltpu.VMEM(begin.shape, begin.dtype),
            pltpu.VMEM((window_rows(ZHI * YS, count), lanes), jnp.bfloat16),
        ],
        compiler_params=params(),
        cost_estimate=cost(tiles, 2),
        name="spread",
    )(place, offsets, counts, views, tiles, begin, base)


def own_view_kernel(place, both, out):
    depth, lanes = out.shape[1], both.shape[2]
    for t in range(out.shape[2] // lanes):
        out[0, :, t * lanes : (t + 1) * lanes] = both[place[2], t * depth : (t + 1) * depth, :]


def own_view(place, both, like):
    return pl.pallas_call(
        own_view_kernel,
        in_specs=[SMEM, VMEM],
        out_specs=VMEM,
        out_shape=jax.ShapeDtypeStruct(like.shape, like.dtype),
        compiler_params=params(),
        cost_estimate=pl.CostEstimate(flops=0, bytes_accessed=8 * like.size, transcendentals=0),
        name="own_view",
    )(place, both)


def swap(array, axis):
    return lax.ppermute(array, axis, [(0, 1), (1, 0)])


def per_device(volume, measured, ray_tiles, tile_offsets, band_counts):
    f32, f16, bf16 = jnp.float32, jnp.float16, jnp.bfloat16
    depth, row_count, width = volume.shape
    tile = ray_tiles.shape[3]
    tile_count = width // tile
    count = tile_count * depth
    zhi, core = lax.axis_index("zhi"), lax.axis_index("core")
    me = lax.axis_index(ANGLE)
    first_row = me * row_count
    gap = lax.axis_size(ANGLE) // ZHI - 1
    is_mine = lax.broadcasted_iota(jnp.int32, (ZHI, 1, 1), 0) == zhi
    place, is_mine, ends_plane, begins_plane = lax.optimization_barrier(
        (jnp.stack([core, first_row, zhi]), is_mine, me == gap, me == gap + 1)
    )

    away, tiles, windows, offsets, counts = load_project(
        place, tile_offsets, band_counts, volume, ray_tiles, PAIR_SCALE
    )
    arrived = swap(away, "core")
    kept = project(place, offsets, counts, windows, tiles, away, PAIR_SCALE)
    pair = (kept + arrived).astype(f16)
    parts = lax.all_to_all(pair, "y", 0, 0, tiled=True)
    plane = jnp.sum(parts.astype(f32), axis=0) * (1 / PAIR_SCALE)
    seen = measured.reshape(depth, tile_count, tile).transpose(1, 0, 2).reshape(count, tile)
    plane = plane - jnp.where(is_mine, seen[None], 0.0)
    far = swap((plane * PLANE_SCALE).astype(f16), "zhi")
    both = plane + far.astype(f32) * (1 / PLANE_SCALE)
    residual = own_view(place, both, measured)
    copies = jnp.broadcast_to(both.astype(bf16)[None], (YS,) + both.shape)
    with_rows = with_row_neighbours(volume, ends_plane, begins_plane)
    views = lax.all_to_all(copies, "y", 0, 0, tiled=True)
    field = jnp.pad(with_slab_neighbours(with_rows).astype(f32), ((0, 0), (0, 0), (1, 1)))
    base = volume.astype(f32) + step_size * smooth_weight * divergence(field)
    views, base, residual = lax.optimization_barrier((views, base, residual))
    views_other = swap(views, "core")
    gradient, tiles = load_spread(place, offsets, counts, views, ray_tiles)
    updated = spread(place, offsets, counts, views_other, tiles, gradient, base)
    return (updated, residual)


def solution(mesh):
    slabs = mesh.shape["slab"]
    fine = Mesh(
        mesh.devices.reshape(slabs // 4, 4, ZHI, YS, CORES), SLAB + ANGLE
    )
    return jax.shard_map(
        per_device,
        mesh=fine,
        in_specs=(
            P(SLAB, ANGLE, None),
            P(ANGLE, SLAB, None),
            P(None, ANGLE, None, None, None),
            P(),
            P(),
        ),
        out_specs=(P(SLAB, ANGLE, None), P(ANGLE, SLAB, None)),
        check_vma=False,
    )
```

```python
from functools import partial

import jax
import jax.numpy as jnp
from jax import lax
from jax.experimental import pallas as pl
from jax.experimental.pallas import tpu as pltpu
from jax.sharding import Mesh, PartitionSpec as P

OFFMAX = 3

step_size = 0.3
smooth_weight = 0.2
smooth_floor = 0.25

ZHI, YS, CORES = 2, 8, 2
SLAB = ("zlo", "x")
ANGLE = ("zhi", "y", "core")

PAIR_SCALE = 2.0**6
PLANE_SCALE = 2.0**3


def shifts_of(size, gap=None):
    up = [(i, i + 1) for i in range(size - 1) if i != gap]
    return up, [(j, i) for i, j in up]


def edges(shard, dim):
    length = shard.shape[dim]
    return lax.slice_in_dim(shard, length - 1, length, axis=dim), lax.slice_in_dim(shard, 0, 1, axis=dim)


def with_row_neighbours(shard, ends_plane, begins_plane):
    size = lax.axis_size(ANGLE)
    gap = size // ZHI - 1
    up, down = shifts_of(size, gap)
    last, first = edges(shard, 1)
    before, after = lax.ppermute(last, ANGLE, up), lax.ppermute(first, ANGLE, down)
    across = lax.ppermute(jnp.where(ends_plane, last, first), ANGLE, [(gap, gap + 1), (gap + 1, gap)])
    before = jnp.where(begins_plane, across, before)
    after = jnp.where(ends_plane, across, after)
    return jnp.concatenate([before, shard, after], axis=1)


def with_slab_neighbours(shard):
    up, down = shifts_of(lax.axis_size(SLAB))
    last, first = edges(shard, 0)
    return jnp.concatenate([lax.ppermute(last, SLAB, up), shard, lax.ppermute(first, SLAB, down)], axis=0)


PAD = 4
GROUP = 4


def copy_rows(count):
    return count + 16 * PAD


def window_rows(bands, count):
    return bands * 2 * copy_rows(count) + count


def band_windows(offset, used, sign, band, bands, count):
    base = band * 2 * copy_rows(count)

    def start(tile):
        return base + tile * 8 + (tile & 1) * (copy_rows(count) - 8)

    first = PAD + sign * (offset - 1)
    second = jnp.where(used > 1, start(first + sign), bands * 2 * copy_rows(count))
    return pl.multiple_of(start(first), 16), pl.multiple_of(second, 16)


def fill_windows(ref, band, wide):
    count, lanes = wide.shape
    rows = copy_rows(count)
    zero = lambda n: jnp.zeros((n, lanes), wide.dtype)
    base = band * 2 * rows
    ref[base : base + rows] = jnp.concatenate([zero(8 * PAD), wide, zero(8 * PAD)], 0).astype(ref.dtype)
    ref[base + rows : base + 2 * rows] = jnp.concatenate(
        [zero(8 * (PAD - 1)), wide, zero(8 * (PAD + 1))], 0
    ).astype(ref.dtype)


def fill_zeros(ref, bands, count):
    base = bands * 2 * copy_rows(count)
    ref[base : base + count] = jnp.zeros((count, ref.shape[1]), ref.dtype)


def angle_of(j, core):
    return ((j % ZHI) * YS + j // ZHI) * CORES + core


def project_one(j, core, first_row, offsets, counts, windows, tiles, out, scale):
    rows = tiles.shape[1]
    count, lanes = out.shape[2:]
    angle = angle_of(j, core)
    pieces = []
    for r in range(rows):
        row = first_row + r
        for start in band_windows(offsets[angle, row], counts[angle, row], 1, r, rows, count):
            pieces.append(windows[pl.ds(start, count), :])
    weights = tiles[angle].reshape(len(pieces) * lanes, lanes)
    view = jnp.dot(jnp.concatenate(pieces, 1), weights, preferred_element_type=jnp.float32)
    out[j // ZHI, j % ZHI] = view * scale


def load_project_kernel(
    place, offsets_hbm, counts_hbm, volume_hbm, tiles_hbm, out, tiles, windows, offsets, counts, volume, tile_sems, sems,
    *, scale
):
    core, first_row = place[0], place[1]
    blocks, rows = ZHI * YS, tiles.shape[1]
    count, lanes = out.shape[2:]
    small = [
        pltpu.make_async_copy(source, target, sems.at[i])
        for i, (source, target) in enumerate(
            ((volume_hbm, volume), (offsets_hbm, offsets), (counts_hbm, counts))
        )
    ]
    copies = tile_copies(tiles_hbm, tiles, tile_sems, 1 - core)
    for copy in small + copies[:blocks]:
        copy.start()
    small[0].wait()
    for r in range(rows):
        line = volume[:, r, :].astype(jnp.float32)
        fill_windows(
            windows, r, jnp.concatenate([line[:, t * lanes : (t + 1) * lanes] for t in range(line.shape[1] // lanes)], 0)
        )
    fill_zeros(windows, rows, count)
    small[1].wait()
    small[2].wait()
    for first in range(0, blocks, GROUP):
        wait_group(copies, first)
        for j in range(first, first + GROUP):
            project_one(j, 1 - core, first_row, offsets, counts, windows, tiles, out, scale)
    for copy in copies[blocks:]:
        copy.wait()


def project_kernel(place, offsets, counts, windows, tiles, out, *, scale):
    for j in range(ZHI * YS):
        project_one(j, place[0], place[1], offsets, counts, windows, tiles, out, scale)


def tile_copies(tiles_hbm, tiles, sems, first_core):
    blocks = ZHI * YS
    order = [angle_of(j, first_core) for j in range(blocks)] + [angle_of(j, 1 - first_core) for j in range(blocks)]
    return [pltpu.make_async_copy(tiles_hbm.at[a], tiles.at[a], sems.at[i]) for i, a in enumerate(order)]


def wait_group(copies, first):
    blocks = ZHI * YS
    for copy in copies[first : first + GROUP]:
        copy.wait()
    if first == 0:
        for copy in copies[blocks:]:
            copy.start()


def spread_group(first, core, first_row, offsets, counts, windows, tiles, begin, out):
    blocks, rows = ZHI * YS, tiles.shape[1]
    count = out.shape[1]
    for r in range(rows):
        row = first_row + r
        lhs, rhs = [], []
        for j in range(first, first + GROUP):
            angle = angle_of(j, core)
            starts = band_windows(offsets[angle, row], counts[angle, row], -1, j, blocks, count)
            for k, start in enumerate(starts):
                lhs.append(windows[pl.ds(start, count), :])
                rhs.append(tiles[angle, r, k])
        part = lax.dot_general(
            jnp.concatenate(lhs, 1),
            jnp.concatenate(rhs, 1),
            (((1,), (1,)), ((), ())),
            preferred_element_type=jnp.float32,
        )
        if first > 0:
            out[r] += part
        elif begin is None:
            out[r] = part
        else:
            out[r] = begin[r] + part


def fill_views(windows, views):
    blocks = ZHI * YS
    for j in range(blocks):
        fill_windows(windows, j, views[j // ZHI, j % ZHI].astype(jnp.float32))
    fill_zeros(windows, blocks, views.shape[2])


def next_x(block):
    width = block.shape[1]
    lane = lax.broadcasted_iota(jnp.int32, block.shape, 1)
    return jnp.where(lane == width - 1, 0.0, pltpu.roll(block, width - 1, 1))


def smooth(field, row):
    wide = lambda i, j: field[i, j].astype(jnp.float32)

    def flow(i, j):
        base = wide(i, j)
        steps = (wide(i + 1, j) - base, wide(i, j + 1) - base, next_x(base) - base)
        inverse = lax.rsqrt(sum(step * step for step in steps) + smooth_floor)
        return [step * inverse for step in steps]

    here = wide(1, row + 1)
    flow_z, flow_y, flow_x = flow(1, row + 1)
    lane = lax.broadcasted_iota(jnp.int32, here.shape, 1)
    edge = here * lax.rsqrt(here * here + smooth_floor)
    before_x = jnp.where(lane == 0, edge, pltpu.roll(flow_x, 1, 1))
    div = flow_z - flow(0, row + 1)[0] + flow_y - flow(1, row)[1] + flow_x - before_x
    return here + step_size * smooth_weight * div


def load_spread_kernel(place, offsets, counts, views, field, tiles_hbm, out, tiles, base, windows, sems):
    copies = tile_copies(tiles_hbm, tiles, sems, place[0])
    for copy in copies[: ZHI * YS]:
        copy.start()
    fill_views(windows, views)
    depth, lanes = field.shape[2], base.shape[2]
    for r in range(base.shape[0]):
        line = smooth(field, r)
        for t in range(line.shape[1] // lanes):
            base[r, t * depth : (t + 1) * depth, :] = line[:, t * lanes : (t + 1) * lanes]
    for first in range(0, ZHI * YS, GROUP):
        wait_group(copies, first)
        spread_group(first, place[0], place[1], offsets, counts, windows, tiles, None, out)
    for copy in copies[ZHI * YS :]:
        copy.wait()


def spread_kernel(place, offsets, counts, views, tiles, begin, base, out, total, windows):
    fill_views(windows, views)
    for first in range(0, ZHI * YS, GROUP):
        spread_group(first, 1 - place[0], place[1], offsets, counts, windows, tiles, begin, total)
    depth, rows, width = out.shape
    lanes = total.shape[2]
    for r in range(rows):
        for t in range(width // lanes):
            some = slice(t * depth, (t + 1) * depth)
            out[:, r, t * lanes : (t + 1) * lanes] = base[r, some, :] - step_size * total[r, some, :]


ANY = pl.BlockSpec(memory_space=pl.ANY)
VMEM = pl.BlockSpec(memory_space=pltpu.VMEM)
SMEM = pl.BlockSpec(memory_space=pltpu.SMEM)


def params():
    return pltpu.CompilerParams(vmem_limit_bytes=16 << 20)


def cost(tiles, share):
    return pl.CostEstimate(
        flops=256 * tiles.size // share, bytes_accessed=2 * tiles.size // share, transcendentals=0
    )


def in_hbm(array):
    return pltpu.with_memory_space_constraint(array, pltpu.HBM)


def load_project(place, offsets, counts, volume, tiles, scale):
    depth, rows, width = volume.shape
    lanes = tiles.shape[-1]
    count = depth * width // lanes
    return pl.pallas_call(
        partial(load_project_kernel, scale=scale),
        in_specs=[SMEM, ANY, ANY, ANY, ANY],
        out_specs=[VMEM, VMEM, VMEM, SMEM, SMEM],
        out_shape=[
            pltpu.VMEM((YS, ZHI, count, lanes), jnp.float32),
            pltpu.VMEM(tiles.shape, tiles.dtype),
            pltpu.VMEM((window_rows(rows, count), lanes), volume.dtype),
            pltpu.SMEM(offsets.shape, offsets.dtype),
            pltpu.SMEM(counts.shape, counts.dtype),
        ],
        scratch_shapes=[
            pltpu.VMEM(volume.shape, volume.dtype),
            pltpu.SemaphoreType.DMA((tiles.shape[0],)),
            pltpu.SemaphoreType.DMA((3,)),
        ],
        compiler_params=params(),
        cost_estimate=cost(tiles, 2),
        name="load_project",
    )(place, in_hbm(offsets), in_hbm(counts), in_hbm(volume), in_hbm(tiles))


def project(place, offsets, counts, windows, tiles, like, scale):
    return pl.pallas_call(
        partial(project_kernel, scale=scale),
        in_specs=[SMEM, SMEM, SMEM, VMEM, VMEM],
        out_specs=VMEM,
        out_shape=pltpu.VMEM(like.shape, jnp.float32),
        compiler_params=params(),
        cost_estimate=cost(tiles, 2),
        name="project",
    )(place, offsets, counts, windows, tiles)


def load_spread(place, offsets, counts, views, field, tiles):
    count, lanes = views.shape[2:]
    lines = (tiles.shape[1], count, lanes)
    return pl.pallas_call(
        load_spread_kernel,
        in_specs=[SMEM, SMEM, SMEM, VMEM, VMEM, ANY],
        out_specs=[VMEM, VMEM, VMEM],
        out_shape=[
            pltpu.VMEM(lines, jnp.float32),
            pltpu.VMEM(tiles.shape, tiles.dtype),
            pltpu.VMEM(lines, jnp.float32),
        ],
        scratch_shapes=[
            pltpu.VMEM((window_rows(ZHI * YS, count), lanes), jnp.bfloat16),
            pltpu.SemaphoreType.DMA((tiles.shape[0],)),
        ],
        compiler_params=params(),
        cost_estimate=cost(tiles, 2),
        name="load_spread",
    )(place, offsets, counts, views, field, in_hbm(tiles))


def spread(place, offsets, counts, views, tiles, begin, base, shape):
    count, lanes = views.shape[2:]
    return pl.pallas_call(
        spread_kernel,
        in_specs=[SMEM, SMEM, SMEM] + [VMEM] * 4,
        out_specs=VMEM,
        out_shape=jax.ShapeDtypeStruct(shape, base.dtype),
        scratch_shapes=[
            pltpu.VMEM(begin.shape, begin.dtype),
            pltpu.VMEM((window_rows(ZHI * YS, count), lanes), jnp.bfloat16),
        ],
        compiler_params=params(),
        cost_estimate=cost(tiles, 2),
        name="spread",
    )(place, offsets, counts, views, tiles, begin, base)


def own_view_kernel(place, both, out):
    depth, lanes = out.shape[1], both.shape[2]
    for t in range(out.shape[2] // lanes):
        out[0, :, t * lanes : (t + 1) * lanes] = both[place[2], t * depth : (t + 1) * depth, :]


def own_view(place, both, like):
    return pl.pallas_call(
        own_view_kernel,
        in_specs=[SMEM, VMEM],
        out_specs=VMEM,
        out_shape=jax.ShapeDtypeStruct(like.shape, like.dtype),
        compiler_params=params(),
        cost_estimate=pl.CostEstimate(flops=0, bytes_accessed=8 * like.size, transcendentals=0),
        name="own_view",
    )(place, both)


def swap(array, axis):
    return lax.ppermute(array, axis, [(0, 1), (1, 0)])


def per_device(volume, measured, ray_tiles, tile_offsets, band_counts):
    f32, f16, bf16 = jnp.float32, jnp.float16, jnp.bfloat16
    depth, row_count, width = volume.shape
    tile = ray_tiles.shape[3]
    tile_count = width // tile
    count = tile_count * depth
    zhi, core = lax.axis_index("zhi"), lax.axis_index("core")
    me = lax.axis_index(ANGLE)
    first_row = me * row_count
    gap = lax.axis_size(ANGLE) // ZHI - 1
    is_mine = lax.broadcasted_iota(jnp.int32, (ZHI, 1, 1), 0) == zhi
    place, is_mine, ends_plane, begins_plane = lax.optimization_barrier(
        (jnp.stack([core, first_row, zhi]), is_mine, me == gap, me == gap + 1)
    )

    away, tiles, windows, offsets, counts = load_project(
        place, tile_offsets, band_counts, volume, ray_tiles, PAIR_SCALE
    )
    arrived = swap(away, "core")
    kept = project(place, offsets, counts, windows, tiles, away, PAIR_SCALE)
    pair = (kept + arrived).astype(f16)
    pair, late_volume = lax.optimization_barrier((pair, volume))
    parts = lax.all_to_all(pair, "y", 0, 0, tiled=True)
    with_rows = with_row_neighbours(late_volume, ends_plane, begins_plane)
    parts, with_rows = lax.optimization_barrier((parts, with_rows))
    plane = jnp.sum(parts.astype(f32), axis=0) * (1 / PAIR_SCALE)
    seen = measured.reshape(depth, tile_count, tile).transpose(1, 0, 2).reshape(count, tile)
    plane = plane - jnp.where(is_mine, seen[None], 0.0)
    far = swap((plane * PLANE_SCALE).astype(f16), "zhi")
    both = plane + far.astype(f32) * (1 / PLANE_SCALE)
    residual = own_view(place, both, measured)
    copies = jnp.broadcast_to(both.astype(bf16)[None], (YS,) + both.shape)
    views = lax.all_to_all(copies, "y", 0, 0, tiled=True)
    beside = with_slab_neighbours(with_rows)
    field = jnp.stack([lax.slice_in_dim(beside, i, i + depth, axis=0) for i in range(3)])
    field = field.transpose(0, 2, 1, 3)
    views, residual, field = lax.optimization_barrier((views, residual, field))
    views_other = swap(views, "core")
    gradient, tiles, base = load_spread(place, offsets, counts, views, field, ray_tiles)
    updated = spread(place, offsets, counts, views_other, tiles, gradient, base, volume.shape)
    return (updated, residual)


def solution(mesh):
    slabs = mesh.shape["slab"]
    fine = Mesh(
        mesh.devices.reshape(slabs // 4, 4, ZHI, YS, CORES), SLAB + ANGLE
    )
    return jax.shard_map(
        per_device,
        mesh=fine,
        in_specs=(
            P(SLAB, ANGLE, None),
            P(ANGLE, SLAB, None),
            P(None, ANGLE, None, None, None),
            P(),
            P(),
        ),
        out_specs=(P(SLAB, ANGLE, None), P(ANGLE, SLAB, None)),
        check_vma=False,
    )
```

```python
from functools import partial

import jax
import jax.numpy as jnp
from jax import lax
from jax.experimental import pallas as pl
from jax.experimental.pallas import tpu as pltpu
from jax.sharding import Mesh, PartitionSpec as P

OFFMAX = 3

step_size = 0.3
smooth_weight = 0.2
smooth_floor = 0.25

ZHI, YS, CORES = 2, 8, 2
SLAB = ("zlo", "x")
ANGLE = ("zhi", "y", "core")

PAIR_SCALE = 2.0**6
PLANE_SCALE = 2.0**3


def shifts_of(size, gap=None):
    up = [(i, i + 1) for i in range(size - 1) if i != gap]
    return up, [(j, i) for i, j in up]


def edges(shard, dim):
    length = shard.shape[dim]
    return lax.slice_in_dim(shard, length - 1, length, axis=dim), lax.slice_in_dim(shard, 0, 1, axis=dim)


def with_row_neighbours(shard, ends_plane, begins_plane):
    size = lax.axis_size(ANGLE)
    gap = size // ZHI - 1
    up, down = shifts_of(size, gap)
    last, first = edges(shard, 1)
    before, after = lax.ppermute(last, ANGLE, up), lax.ppermute(first, ANGLE, down)
    across = lax.ppermute(jnp.where(ends_plane, last, first), ANGLE, [(gap, gap + 1), (gap + 1, gap)])
    before = jnp.where(begins_plane, across, before)
    after = jnp.where(ends_plane, across, after)
    return jnp.concatenate([before, shard, after], axis=1)


def with_slab_neighbours(shard):
    up, down = shifts_of(lax.axis_size(SLAB))
    last, first = edges(shard, 0)
    return jnp.concatenate([lax.ppermute(last, SLAB, up), shard, lax.ppermute(first, SLAB, down)], axis=0)


PAD = 4
GROUP = 4
BLOCKS = ZHI * YS
EARLY = 12


def copy_rows(count):
    return count + 16 * PAD


def window_rows(bands, count):
    return bands * 2 * copy_rows(count) + count


def band_windows(offset, used, sign, band, bands, count):
    base = band * 2 * copy_rows(count)

    def start(tile):
        return base + tile * 8 + (tile & 1) * (copy_rows(count) - 8)

    first = PAD + sign * (offset - 1)
    second = jnp.where(used > 1, start(first + sign), bands * 2 * copy_rows(count))
    return pl.multiple_of(start(first), 16), pl.multiple_of(second, 16)


def fill_windows(ref, band, wide):
    count, lanes = wide.shape
    rows = copy_rows(count)
    zero = lambda n: jnp.zeros((n, lanes), wide.dtype)
    base = band * 2 * rows
    ref[base : base + rows] = jnp.concatenate([zero(8 * PAD), wide, zero(8 * PAD)], 0).astype(ref.dtype)
    ref[base + rows : base + 2 * rows] = jnp.concatenate(
        [zero(8 * (PAD - 1)), wide, zero(8 * (PAD + 1))], 0
    ).astype(ref.dtype)


def fill_zeros(ref, bands, count):
    base = bands * 2 * copy_rows(count)
    ref[base : base + count] = jnp.zeros((count, ref.shape[1]), ref.dtype)


def angle_of(j, core):
    return ((j % ZHI) * YS + j // ZHI) * CORES + core


def project_one(j, core, first_row, offsets, counts, windows, tiles, out, scale):
    rows = tiles.shape[1]
    count, lanes = out.shape[2:]
    angle = angle_of(j, core)
    pieces = []
    for r in range(rows):
        row = first_row + r
        for start in band_windows(offsets[angle, row], counts[angle, row], 1, r, rows, count):
            pieces.append(windows[pl.ds(start, count), :])
    weights = tiles[angle].reshape(len(pieces) * lanes, lanes)
    view = jnp.dot(jnp.concatenate(pieces, 1), weights, preferred_element_type=jnp.float32)
    out[j // ZHI, j % ZHI] = view * scale


def load_project_kernel(
    place, offsets_hbm, counts_hbm, volume_hbm, tiles_hbm, out, tiles, windows, offsets, counts, volume, tile_sems, sems,
    *, scale
):
    core, first_row = place[0], place[1]
    blocks, rows = ZHI * YS, tiles.shape[1]
    count, lanes = out.shape[2:]
    small = [
        pltpu.make_async_copy(source, target, sems.at[i])
        for i, (source, target) in enumerate(
            ((volume_hbm, volume), (offsets_hbm, offsets), (counts_hbm, counts))
        )
    ]
    copies = tile_copies(tiles_hbm, tiles, tile_sems, 1 - core)
    for copy in small + copies[:blocks]:
        copy.start()
    small[0].wait()
    for r in range(rows):
        line = volume[:, r, :].astype(jnp.float32)
        fill_windows(
            windows, r, jnp.concatenate([line[:, t * lanes : (t + 1) * lanes] for t in range(line.shape[1] // lanes)], 0)
        )
    fill_zeros(windows, rows, count)
    small[1].wait()
    small[2].wait()
    for first in range(0, blocks, GROUP):
        wait_group(copies, first)
        for j in range(first, first + GROUP):
            project_one(j, 1 - core, first_row, offsets, counts, windows, tiles, out, scale)
    for copy in copies[blocks:]:
        copy.wait()


def project_kernel(place, offsets, counts, windows, tiles, out, *, scale):
    for j in range(ZHI * YS):
        project_one(j, place[0], place[1], offsets, counts, windows, tiles, out, scale)


def tile_copies(tiles_hbm, tiles, sems, first_core):
    order = [angle_of(j, first_core) for j in range(BLOCKS)] + [angle_of(j, 1 - first_core) for j in range(BLOCKS)]
    return [pltpu.make_async_copy(tiles_hbm.at[a], tiles.at[a], sems.at[i]) for i, a in enumerate(order)]


def block_copies(tiles_hbm, tiles, sems, core, blocks, place=0):
    return [
        pltpu.make_async_copy(tiles_hbm.at[angle_of(j, core)], tiles.at[place + i], sems.at[place + i])
        for i, j in enumerate(blocks)
    ]


def wait_group(copies, first):
    blocks = ZHI * YS
    for copy in copies[first : first + GROUP]:
        copy.wait()
    if first == 0:
        for copy in copies[blocks:]:
            copy.start()


def spread_group(first, core, first_row, offsets, counts, windows, tiles, begin, out):
    blocks, rows = BLOCKS, tiles.shape[1]
    count = out.shape[1]
    for r in range(rows):
        row = first_row + r
        lhs, rhs = [], []
        for j in range(first, first + GROUP):
            angle = angle_of(j, core)
            starts = band_windows(offsets[angle, row], counts[angle, row], -1, j, blocks, count)
            for k, start in enumerate(starts):
                lhs.append(windows[pl.ds(start, count), :])
                rhs.append(tiles[j - first, r, k])
        part = lax.dot_general(
            jnp.concatenate(lhs, 1),
            jnp.concatenate(rhs, 1),
            (((1,), (1,)), ((), ())),
            preferred_element_type=jnp.float32,
        )
        if first > 0:
            out[r] += part
        elif begin is None:
            out[r] = part
        else:
            out[r] = begin[r] + part


def fill_views(windows, views):
    blocks = ZHI * YS
    for j in range(blocks):
        fill_windows(windows, j, views[j // ZHI, j % ZHI].astype(jnp.float32))
    fill_zeros(windows, blocks, views.shape[2])


def next_x(block):
    width = block.shape[1]
    lane = lax.broadcasted_iota(jnp.int32, block.shape, 1)
    return jnp.where(lane == width - 1, 0.0, pltpu.roll(block, width - 1, 1))


def smooth(field, row):
    wide = lambda i, j: field[i, j].astype(jnp.float32)

    def flow(i, j):
        base = wide(i, j)
        steps = (wide(i + 1, j) - base, wide(i, j + 1) - base, next_x(base) - base)
        inverse = lax.rsqrt(sum(step * step for step in steps) + smooth_floor)
        return [step * inverse for step in steps]

    here = wide(1, row + 1)
    flow_z, flow_y, flow_x = flow(1, row + 1)
    lane = lax.broadcasted_iota(jnp.int32, here.shape, 1)
    edge = here * lax.rsqrt(here * here + smooth_floor)
    before_x = jnp.where(lane == 0, edge, pltpu.roll(flow_x, 1, 1))
    div = flow_z - flow(0, row + 1)[0] + flow_y - flow(1, row)[1] + flow_x - before_x
    return here + step_size * smooth_weight * div


def load_spread_kernel(place, offsets, counts, views, early, tiles_hbm, out, later, windows, tiles, sems, later_sems):
    now = block_copies(tiles_hbm, tiles, sems, place[0], range(EARLY, BLOCKS))
    then = block_copies(tiles_hbm, later, later_sems, 1 - place[0], range(BLOCKS))
    for copy in now + then:
        copy.start()
    fill_views(windows, views)
    for first in range(0, BLOCKS, GROUP):
        if first == EARLY:
            for copy in now:
                copy.wait()
        group = early.at[pl.ds(first, GROUP)] if first < EARLY else tiles.at[pl.ds(first - EARLY, GROUP)]
        spread_group(first, place[0], place[1], offsets, counts, windows, group, None, out)
    for copy in then:
        copy.wait()


def spread_kernel(place, offsets, counts, views, tiles, begin, base, out, total, windows):
    fill_views(windows, views)
    for first in range(0, BLOCKS, GROUP):
        group = tiles.at[pl.ds(first, GROUP)]
        spread_group(first, 1 - place[0], place[1], offsets, counts, windows, group, begin, total)
    depth, rows, width = out.shape
    lanes = total.shape[2]
    for r in range(rows):
        for t in range(width // lanes):
            some = slice(t * depth, (t + 1) * depth)
            out[:, r, t * lanes : (t + 1) * lanes] = base[r, some, :] - step_size * total[r, some, :]


ANY = pl.BlockSpec(memory_space=pl.ANY)
VMEM = pl.BlockSpec(memory_space=pltpu.VMEM)
SMEM = pl.BlockSpec(memory_space=pltpu.SMEM)


def params():
    return pltpu.CompilerParams(vmem_limit_bytes=16 << 20)


def cost(tiles, share):
    return pl.CostEstimate(
        flops=256 * tiles.size // share, bytes_accessed=2 * tiles.size // share, transcendentals=0
    )


def in_hbm(array):
    return pltpu.with_memory_space_constraint(array, pltpu.HBM)


def load_project(place, offsets, counts, volume, tiles, scale):
    depth, rows, width = volume.shape
    lanes = tiles.shape[-1]
    count = depth * width // lanes
    return pl.pallas_call(
        partial(load_project_kernel, scale=scale),
        in_specs=[SMEM, ANY, ANY, ANY, ANY],
        out_specs=[VMEM, VMEM, VMEM, SMEM, SMEM],
        out_shape=[
            pltpu.VMEM((YS, ZHI, count, lanes), jnp.float32),
            pltpu.VMEM(tiles.shape, tiles.dtype),
            pltpu.VMEM((window_rows(rows, count), lanes), volume.dtype),
            pltpu.SMEM(offsets.shape, offsets.dtype),
            pltpu.SMEM(counts.shape, counts.dtype),
        ],
        scratch_shapes=[
            pltpu.VMEM(volume.shape, volume.dtype),
            pltpu.SemaphoreType.DMA((tiles.shape[0],)),
            pltpu.SemaphoreType.DMA((3,)),
        ],
        compiler_params=params(),
        cost_estimate=cost(tiles, 2),
        name="load_project",
    )(place, in_hbm(offsets), in_hbm(counts), in_hbm(volume), in_hbm(tiles))


def project(place, offsets, counts, windows, tiles, like, scale):
    return pl.pallas_call(
        partial(project_kernel, scale=scale),
        in_specs=[SMEM, SMEM, SMEM, VMEM, VMEM],
        out_specs=VMEM,
        out_shape=pltpu.VMEM(like.shape, jnp.float32),
        compiler_params=params(),
        cost_estimate=cost(tiles, 2),
        name="project",
    )(place, offsets, counts, windows, tiles)


def load_spread(place, offsets, counts, views, early, tiles):
    count, lanes = views.shape[2:]
    lines = (tiles.shape[1], count, lanes)
    return pl.pallas_call(
        load_spread_kernel,
        in_specs=[SMEM, SMEM, SMEM, VMEM, VMEM, ANY],
        out_specs=[VMEM, VMEM],
        out_shape=[
            pltpu.VMEM(lines, jnp.float32),
            pltpu.VMEM((BLOCKS,) + tiles.shape[1:], tiles.dtype),
        ],
        scratch_shapes=[
            pltpu.VMEM((window_rows(ZHI * YS, count), lanes), jnp.bfloat16),
            pltpu.VMEM((BLOCKS - EARLY,) + tiles.shape[1:], tiles.dtype),
            pltpu.SemaphoreType.DMA((BLOCKS - EARLY,)),
            pltpu.SemaphoreType.DMA((BLOCKS,)),
        ],
        compiler_params=params(),
        cost_estimate=cost(tiles, 2),
        name="load_spread",
    )(place, offsets, counts, views, early, in_hbm(tiles))


def spread(place, offsets, counts, views, tiles, begin, base, shape):
    count, lanes = views.shape[2:]
    return pl.pallas_call(
        spread_kernel,
        in_specs=[SMEM, SMEM, SMEM] + [VMEM] * 4,
        out_specs=VMEM,
        out_shape=jax.ShapeDtypeStruct(shape, base.dtype),
        scratch_shapes=[
            pltpu.VMEM(begin.shape, begin.dtype),
            pltpu.VMEM((window_rows(ZHI * YS, count), lanes), jnp.bfloat16),
        ],
        compiler_params=params(),
        cost_estimate=cost(tiles, 2),
        name="spread",
    )(place, offsets, counts, views, tiles, begin, base)


def close_window_kernel(place, both, field, tiles_hbm, out, early, base, sems):
    copies = block_copies(tiles_hbm, early, sems, place[0], range(EARLY))
    for copy in copies:
        copy.start()
    depth, lanes = out.shape[1], both.shape[2]
    for t in range(out.shape[2] // lanes):
        out[0, :, t * lanes : (t + 1) * lanes] = both[place[2], t * depth : (t + 1) * depth, :]
    for r in range(base.shape[0]):
        line = smooth(field, r)
        for t in range(line.shape[1] // lanes):
            base[r, t * depth : (t + 1) * depth, :] = line[:, t * lanes : (t + 1) * lanes]
    for copy in copies:
        copy.wait()


def close_window(place, both, field, tiles, like):
    return pl.pallas_call(
        close_window_kernel,
        in_specs=[SMEM, VMEM, VMEM, ANY],
        out_specs=[VMEM, VMEM, VMEM],
        out_shape=[
            jax.ShapeDtypeStruct(like.shape, like.dtype),
            pltpu.VMEM((EARLY,) + tiles.shape[1:], tiles.dtype),
            pltpu.VMEM((tiles.shape[1],) + both.shape[1:], both.dtype),
        ],
        scratch_shapes=[pltpu.SemaphoreType.DMA((EARLY,))],
        compiler_params=params(),
        cost_estimate=pl.CostEstimate(flops=0, bytes_accessed=8 * like.size, transcendentals=0),
        name="close_window",
    )(place, both, field, in_hbm(tiles))


def swap(array, axis):
    return lax.ppermute(array, axis, [(0, 1), (1, 0)])


def per_device(volume, measured, ray_tiles, tile_offsets, band_counts):
    f32, f16, bf16 = jnp.float32, jnp.float16, jnp.bfloat16
    depth, row_count, width = volume.shape
    tile = ray_tiles.shape[3]
    tile_count = width // tile
    count = tile_count * depth
    zhi, core = lax.axis_index("zhi"), lax.axis_index("core")
    me = lax.axis_index(ANGLE)
    first_row = me * row_count
    gap = lax.axis_size(ANGLE) // ZHI - 1
    is_mine = lax.broadcasted_iota(jnp.int32, (ZHI, 1, 1), 0) == zhi
    place, is_mine, ends_plane, begins_plane = lax.optimization_barrier(
        (jnp.stack([core, first_row, zhi]), is_mine, me == gap, me == gap + 1)
    )

    away, tiles, windows, offsets, counts = load_project(
        place, tile_offsets, band_counts, volume, ray_tiles, PAIR_SCALE
    )
    arrived = swap(away, "core")
    kept = project(place, offsets, counts, windows, tiles, away, PAIR_SCALE)
    pair = (kept + arrived).astype(f16)
    pair, late_volume = lax.optimization_barrier((pair, volume))
    parts = lax.all_to_all(pair, "y", 0, 0, tiled=True)
    with_rows = with_row_neighbours(late_volume, ends_plane, begins_plane)
    parts, with_rows = lax.optimization_barrier((parts, with_rows))
    plane = jnp.sum(parts.astype(f32), axis=0) * (1 / PAIR_SCALE)
    seen = measured.reshape(depth, tile_count, tile).transpose(1, 0, 2).reshape(count, tile)
    plane = plane - jnp.where(is_mine, seen[None], 0.0)
    far = swap((plane * PLANE_SCALE).astype(f16), "zhi")
    both = plane + far.astype(f32) * (1 / PLANE_SCALE)
    copies = jnp.broadcast_to(both.astype(bf16)[None], (YS,) + both.shape)
    views = lax.all_to_all(copies, "y", 0, 0, tiled=True)
    beside = with_slab_neighbours(with_rows)
    field = jnp.stack([lax.slice_in_dim(beside, i, i + depth, axis=0) for i in range(3)])
    field = field.transpose(0, 2, 1, 3)
    residual, early, base = close_window(place, both, field, ray_tiles, measured)
    views, residual, early, base = lax.optimization_barrier((views, residual, early, base))
    views_other = swap(views, "core")
    gradient, tiles = load_spread(place, offsets, counts, views, early, ray_tiles)
    updated = spread(place, offsets, counts, views_other, tiles, gradient, base, volume.shape)
    return (updated, residual)


def solution(mesh):
    slabs = mesh.shape["slab"]
    fine = Mesh(
        mesh.devices.reshape(slabs // 4, 4, ZHI, YS, CORES), SLAB + ANGLE
    )
    return jax.shard_map(
        per_device,
        mesh=fine,
        in_specs=(
            P(SLAB, ANGLE, None),
            P(ANGLE, SLAB, None),
            P(None, ANGLE, None, None, None),
            P(),
            P(),
        ),
        out_specs=(P(SLAB, ANGLE, None), P(ANGLE, SLAB, None)),
        check_vma=False,
    )
```

```python
from functools import partial

import jax
import jax.numpy as jnp
from jax import lax
from jax.experimental import pallas as pl
from jax.experimental.pallas import tpu as pltpu
from jax.sharding import Mesh, PartitionSpec as P

OFFMAX = 3

step_size = 0.3
smooth_weight = 0.2
smooth_floor = 0.25

ZHI, YS, CORES = 2, 8, 2
SLAB = ("zlo", "x")
ANGLE = ("zhi", "y", "core")

PAIR_SCALE = 2.0**6
PLANE_SCALE = 2.0**3


def shifts_of(size, gap=None):
    up = [(i, i + 1) for i in range(size - 1) if i != gap]
    return up, [(j, i) for i, j in up]


def edges(shard, dim):
    length = shard.shape[dim]
    return lax.slice_in_dim(shard, length - 1, length, axis=dim), lax.slice_in_dim(shard, 0, 1, axis=dim)


def with_row_neighbours(shard, ends_plane, begins_plane):
    size = lax.axis_size(ANGLE)
    gap = size // ZHI - 1
    up, down = shifts_of(size, gap)
    last, first = edges(shard, 1)
    before, after = lax.ppermute(last, ANGLE, up), lax.ppermute(first, ANGLE, down)
    across = lax.ppermute(jnp.where(ends_plane, last, first), ANGLE, [(gap, gap + 1), (gap + 1, gap)])
    before = jnp.where(begins_plane, across, before)
    after = jnp.where(ends_plane, across, after)
    return jnp.concatenate([before, shard, after], axis=1)


def with_slab_neighbours(shard):
    up, down = shifts_of(lax.axis_size(SLAB))
    last, first = edges(shard, 0)
    return jnp.concatenate([lax.ppermute(last, SLAB, up), shard, lax.ppermute(first, SLAB, down)], axis=0)


PAD = 4
GROUP = 4
BLOCKS = ZHI * YS


def copy_rows(count):
    return count + 16 * PAD


def window_rows(bands, count):
    return bands * 2 * copy_rows(count) + count


def band_windows(offset, used, sign, band, bands, count):
    base = band * 2 * copy_rows(count)

    def start(tile):
        return base + tile * 8 + (tile & 1) * (copy_rows(count) - 8)

    first = PAD + sign * (offset - 1)
    second = jnp.where(used > 1, start(first + sign), bands * 2 * copy_rows(count))
    return pl.multiple_of(start(first), 16), pl.multiple_of(second, 16)


def fill_windows(ref, band, wide):
    count, lanes = wide.shape
    rows = copy_rows(count)
    zero = lambda n: jnp.zeros((n, lanes), wide.dtype)
    base = band * 2 * rows
    ref[base : base + rows] = jnp.concatenate([zero(8 * PAD), wide, zero(8 * PAD)], 0).astype(ref.dtype)
    ref[base + rows : base + 2 * rows] = jnp.concatenate(
        [zero(8 * (PAD - 1)), wide, zero(8 * (PAD + 1))], 0
    ).astype(ref.dtype)


def fill_zeros(ref, bands, count):
    base = bands * 2 * copy_rows(count)
    ref[base : base + count] = jnp.zeros((count, ref.shape[1]), ref.dtype)


def angle_of(j, core):
    return ((j % ZHI) * YS + j // ZHI) * CORES + core


def project_one(j, core, first_row, offsets, counts, windows, tiles, out, scale):
    rows = tiles.shape[2]
    count, lanes = out.shape[2:]
    angle = angle_of(j, core)
    pieces = []
    for r in range(rows):
        row = first_row + r
        for start in band_windows(offsets[angle, row], counts[angle, row], 1, r, rows, count):
            pieces.append(windows[pl.ds(start, count), :])
    weights = tiles[j % ZHI, j // ZHI].reshape(len(pieces) * lanes, lanes)
    view = jnp.dot(jnp.concatenate(pieces, 1), weights, preferred_element_type=jnp.float32)
    out[j // ZHI, j % ZHI] = view * scale


def load_project_kernel(
    place, offsets_hbm, counts_hbm, volume_hbm, tiles_hbm, out, later, windows, offsets, counts, volume, tiles, sems, more_sems,
    *, scale
):
    core, first_row = place[0], place[1]
    rows = tiles.shape[2]
    count, lanes = out.shape[2:]
    small = [
        pltpu.make_async_copy(source, target, more_sems.at[i])
        for i, (source, target) in enumerate(
            ((volume_hbm, volume), (offsets_hbm, offsets), (counts_hbm, counts))
        )
    ]
    now = group_copies(tiles_hbm, tiles, sems, 1 - core)
    then = tile_copy(tiles_hbm, later, more_sems.at[len(small)], core, 0, BLOCKS)
    for copy in small + now:
        copy.start()
    small[0].wait()
    for r in range(rows):
        line = volume[:, r, :].astype(jnp.float32)
        fill_windows(
            windows, r, jnp.concatenate([line[:, t * lanes : (t + 1) * lanes] for t in range(line.shape[1] // lanes)], 0)
        )
    fill_zeros(windows, rows, count)
    small[1].wait()
    small[2].wait()
    for i, first in enumerate(range(0, BLOCKS, GROUP)):
        now[i].wait()
        if i == 0:
            then.start()
        for j in range(first, first + GROUP):
            project_one(j, 1 - core, first_row, offsets, counts, windows, tiles, out, scale)
    then.wait()


def project_kernel(place, offsets, counts, windows, tiles, out, *, scale):
    for j in range(ZHI * YS):
        project_one(j, place[0], place[1], offsets, counts, windows, tiles, out, scale)


def tile_copy(tiles_hbm, tiles, sem, core, first, end):
    by_core = tiles_hbm.reshape((ZHI, YS, CORES) + tuple(tiles_hbm.shape[1:]))
    ys = pl.ds(first // ZHI, (end - first) // ZHI)
    return pltpu.make_async_copy(by_core.at[:, ys, core], tiles.at[:, ys], sem)


def group_copies(tiles_hbm, tiles, sems, core):
    return [
        tile_copy(tiles_hbm, tiles, sems.at[i], core, first, first + GROUP)
        for i, first in enumerate(range(0, BLOCKS, GROUP))
    ]


def tiles_of(tiles):
    return (ZHI, YS) + tuple(tiles.shape[1:])


def spread_group(first, core, first_row, offsets, counts, windows, tiles, begin, out):
    blocks, rows = BLOCKS, tiles.shape[2]
    count = out.shape[1]
    for r in range(rows):
        row = first_row + r
        lhs, rhs = [], []
        for j in range(first, first + GROUP):
            angle = angle_of(j, core)
            starts = band_windows(offsets[angle, row], counts[angle, row], -1, j, blocks, count)
            for k, start in enumerate(starts):
                lhs.append(windows[pl.ds(start, count), :])
                rhs.append(tiles[j % ZHI, j // ZHI, r, k])
        part = lax.dot_general(
            jnp.concatenate(lhs, 1),
            jnp.concatenate(rhs, 1),
            (((1,), (1,)), ((), ())),
            preferred_element_type=jnp.float32,
        )
        if first > 0:
            out[r] += part
        elif begin is None:
            out[r] = part
        else:
            out[r] = begin[r] + part


def fill_views(windows, views):
    blocks = ZHI * YS
    for j in range(blocks):
        fill_windows(windows, j, views[j // ZHI, j % ZHI].astype(jnp.float32))
    fill_zeros(windows, blocks, views.shape[2])


def next_x(block):
    width = block.shape[1]
    lane = lax.broadcasted_iota(jnp.int32, block.shape, 1)
    return jnp.where(lane == width - 1, 0.0, pltpu.roll(block, width - 1, 1))


def smooth(field, row):
    wide = lambda i, j: field[i, j].astype(jnp.float32)

    def flow(i, j):
        base = wide(i, j)
        steps = (wide(i + 1, j) - base, wide(i, j + 1) - base, next_x(base) - base)
        inverse = lax.rsqrt(sum(step * step for step in steps) + smooth_floor)
        return [step * inverse for step in steps]

    here = wide(1, row + 1)
    flow_z, flow_y, flow_x = flow(1, row + 1)
    lane = lax.broadcasted_iota(jnp.int32, here.shape, 1)
    edge = here * lax.rsqrt(here * here + smooth_floor)
    before_x = jnp.where(lane == 0, edge, pltpu.roll(flow_x, 1, 1))
    div = flow_z - flow(0, row + 1)[0] + flow_y - flow(1, row)[1] + flow_x - before_x
    return here + step_size * smooth_weight * div


def load_spread_kernel(place, offsets, counts, views, field, tiles_hbm, out, later, base, windows, tiles, sems, later_sem):
    now = group_copies(tiles_hbm, tiles, sems, place[0])
    then = tile_copy(tiles_hbm, later, later_sem, 1 - place[0], 0, BLOCKS)
    for copy in now:
        copy.start()
    fill_views(windows, views)
    depth, lanes = field.shape[2], base.shape[2]
    for r in range(base.shape[0]):
        line = smooth(field, r)
        for t in range(line.shape[1] // lanes):
            base[r, t * depth : (t + 1) * depth, :] = line[:, t * lanes : (t + 1) * lanes]
    for i, first in enumerate(range(0, BLOCKS, GROUP)):
        now[i].wait()
        if i == 0:
            then.start()
        spread_group(first, place[0], place[1], offsets, counts, windows, tiles, None, out)
    then.wait()


def spread_kernel(place, offsets, counts, views, tiles, begin, base, out, total, windows):
    fill_views(windows, views)
    for first in range(0, ZHI * YS, GROUP):
        spread_group(first, 1 - place[0], place[1], offsets, counts, windows, tiles, begin, total)
    depth, rows, width = out.shape
    lanes = total.shape[2]
    for r in range(rows):
        for t in range(width // lanes):
            some = slice(t * depth, (t + 1) * depth)
            out[:, r, t * lanes : (t + 1) * lanes] = base[r, some, :] - step_size * total[r, some, :]


ANY = pl.BlockSpec(memory_space=pl.ANY)
VMEM = pl.BlockSpec(memory_space=pltpu.VMEM)
SMEM = pl.BlockSpec(memory_space=pltpu.SMEM)


def params():
    return pltpu.CompilerParams(vmem_limit_bytes=16 << 20)


def cost(tiles, share):
    return pl.CostEstimate(
        flops=256 * tiles.size // share, bytes_accessed=2 * tiles.size // share, transcendentals=0
    )


def in_hbm(array):
    return pltpu.with_memory_space_constraint(array, pltpu.HBM)


def load_project(place, offsets, counts, volume, tiles, scale):
    depth, rows, width = volume.shape
    lanes = tiles.shape[-1]
    count = depth * width // lanes
    return pl.pallas_call(
        partial(load_project_kernel, scale=scale),
        in_specs=[SMEM, ANY, ANY, ANY, ANY],
        out_specs=[VMEM, VMEM, VMEM, SMEM, SMEM],
        out_shape=[
            pltpu.VMEM((YS, ZHI, count, lanes), jnp.float32),
            pltpu.VMEM(tiles_of(tiles), tiles.dtype),
            pltpu.VMEM((window_rows(rows, count), lanes), volume.dtype),
            pltpu.SMEM(offsets.shape, offsets.dtype),
            pltpu.SMEM(counts.shape, counts.dtype),
        ],
        scratch_shapes=[
            pltpu.VMEM(volume.shape, volume.dtype),
            pltpu.VMEM(tiles_of(tiles), tiles.dtype),
            pltpu.SemaphoreType.DMA((BLOCKS // GROUP,)),
            pltpu.SemaphoreType.DMA((4,)),
        ],
        compiler_params=params(),
        cost_estimate=cost(tiles, 2),
        name="load_project",
    )(place, in_hbm(offsets), in_hbm(counts), in_hbm(volume), in_hbm(tiles))


def project(place, offsets, counts, windows, tiles, like, scale):
    return pl.pallas_call(
        partial(project_kernel, scale=scale),
        in_specs=[SMEM, SMEM, SMEM, VMEM, VMEM],
        out_specs=VMEM,
        out_shape=pltpu.VMEM(like.shape, jnp.float32),
        compiler_params=params(),
        cost_estimate=cost(tiles, 2),
        name="project",
    )(place, offsets, counts, windows, tiles)


def load_spread(place, offsets, counts, views, field, tiles):
    count, lanes = views.shape[2:]
    lines = (tiles.shape[1], count, lanes)
    return pl.pallas_call(
        load_spread_kernel,
        in_specs=[SMEM, SMEM, SMEM, VMEM, VMEM, ANY],
        out_specs=[VMEM, VMEM, VMEM],
        out_shape=[
            pltpu.VMEM(lines, jnp.float32),
            pltpu.VMEM(tiles_of(tiles), tiles.dtype),
            pltpu.VMEM(lines, jnp.float32),
        ],
        scratch_shapes=[
            pltpu.VMEM((window_rows(ZHI * YS, count), lanes), jnp.bfloat16),
            pltpu.VMEM(tiles_of(tiles), tiles.dtype),
            pltpu.SemaphoreType.DMA((BLOCKS // GROUP,)),
            pltpu.SemaphoreType.DMA,
        ],
        compiler_params=params(),
        cost_estimate=cost(tiles, 2),
        name="load_spread",
    )(place, offsets, counts, views, field, in_hbm(tiles))


def spread(place, offsets, counts, views, tiles, begin, base, shape):
    count, lanes = views.shape[2:]
    return pl.pallas_call(
        spread_kernel,
        in_specs=[SMEM, SMEM, SMEM] + [VMEM] * 4,
        out_specs=VMEM,
        out_shape=jax.ShapeDtypeStruct(shape, base.dtype),
        scratch_shapes=[
            pltpu.VMEM(begin.shape, begin.dtype),
            pltpu.VMEM((window_rows(ZHI * YS, count), lanes), jnp.bfloat16),
        ],
        compiler_params=params(),
        cost_estimate=cost(tiles, 2),
        name="spread",
    )(place, offsets, counts, views, tiles, begin, base)


def own_view_kernel(place, both, out):
    depth, lanes = out.shape[1], both.shape[2]
    for t in range(out.shape[2] // lanes):
        out[0, :, t * lanes : (t + 1) * lanes] = both[place[2], t * depth : (t + 1) * depth, :]


def own_view(place, both, like):
    return pl.pallas_call(
        own_view_kernel,
        in_specs=[SMEM, VMEM],
        out_specs=VMEM,
        out_shape=jax.ShapeDtypeStruct(like.shape, like.dtype),
        compiler_params=params(),
        cost_estimate=pl.CostEstimate(flops=0, bytes_accessed=8 * like.size, transcendentals=0),
        name="own_view",
    )(place, both)


def swap(array, axis):
    return lax.ppermute(array, axis, [(0, 1), (1, 0)])


def per_device(volume, measured, ray_tiles, tile_offsets, band_counts):
    f32, f16, bf16 = jnp.float32, jnp.float16, jnp.bfloat16
    depth, row_count, width = volume.shape
    tile = ray_tiles.shape[3]
    tile_count = width // tile
    count = tile_count * depth
    zhi, core = lax.axis_index("zhi"), lax.axis_index("core")
    me = lax.axis_index(ANGLE)
    first_row = me * row_count
    gap = lax.axis_size(ANGLE) // ZHI - 1
    is_mine = lax.broadcasted_iota(jnp.int32, (ZHI, 1, 1), 0) == zhi
    place, is_mine, ends_plane, begins_plane = lax.optimization_barrier(
        (jnp.stack([core, first_row, zhi]), is_mine, me == gap, me == gap + 1)
    )

    away, tiles, windows, offsets, counts = load_project(
        place, tile_offsets, band_counts, volume, ray_tiles, PAIR_SCALE
    )
    arrived = swap(away, "core")
    kept = project(place, offsets, counts, windows, tiles, away, PAIR_SCALE)
    pair = (kept + arrived).astype(f16)
    pair, late_volume = lax.optimization_barrier((pair, volume))
    parts = lax.all_to_all(pair, "y", 0, 0, tiled=True)
    with_rows = with_row_neighbours(late_volume, ends_plane, begins_plane)
    parts, with_rows = lax.optimization_barrier((parts, with_rows))
    plane = jnp.sum(parts.astype(f32), axis=0) * (1 / PAIR_SCALE)
    seen = measured.reshape(depth, tile_count, tile).transpose(1, 0, 2).reshape(count, tile)
    plane = plane - jnp.where(is_mine, seen[None], 0.0)
    far = swap((plane * PLANE_SCALE).astype(f16), "zhi")
    both = plane + far.astype(f32) * (1 / PLANE_SCALE)
    residual = own_view(place, both, measured)
    copies = jnp.broadcast_to(both.astype(bf16)[None], (YS,) + both.shape)
    views = lax.all_to_all(copies, "y", 0, 0, tiled=True)
    beside = with_slab_neighbours(with_rows)
    field = jnp.stack([lax.slice_in_dim(beside, i, i + depth, axis=0) for i in range(3)])
    field = field.transpose(0, 2, 1, 3)
    views, residual, field = lax.optimization_barrier((views, residual, field))
    views_other = swap(views, "core")
    gradient, tiles, base = load_spread(place, offsets, counts, views, field, ray_tiles)
    updated = spread(place, offsets, counts, views_other, tiles, gradient, base, volume.shape)
    return (updated, residual)


def solution(mesh):
    slabs = mesh.shape["slab"]
    fine = Mesh(
        mesh.devices.reshape(slabs // 4, 4, ZHI, YS, CORES), SLAB + ANGLE
    )
    return jax.shard_map(
        per_device,
        mesh=fine,
        in_specs=(
            P(SLAB, ANGLE, None),
            P(ANGLE, SLAB, None),
            P(None, ANGLE, None, None, None),
            P(),
            P(),
        ),
        out_specs=(P(SLAB, ANGLE, None), P(ANGLE, SLAB, None)),
        check_vma=False,
    )
```

```python
import jax
import jax.numpy as jnp
from jax import lax
from jax.experimental import pallas as pl
from jax.experimental.pallas import tpu as pltpu
from jax.sharding import Mesh, PartitionSpec as P

OFFMAX = 3

step_size = 0.3
smooth_weight = 0.2
smooth_floor = 0.25

ZHI, YS, CORES = 2, 8, 2
SLAB = ("zlo", "x")
ANGLE = ("zhi", "y", "core")

def shifts_of(size, gap=None):
    up = [(i, i + 1) for i in range(size - 1) if i != gap]
    return up, [(j, i) for i, j in up]


def edges(shard, dim):
    length = shard.shape[dim]
    return lax.slice_in_dim(shard, length - 1, length, axis=dim), lax.slice_in_dim(shard, 0, 1, axis=dim)


def with_row_neighbours(shard, ends_plane, begins_plane):
    size = lax.axis_size(ANGLE)
    gap = size // ZHI - 1
    up, down = shifts_of(size, gap)
    last, first = edges(shard, 1)
    before, after = lax.ppermute(last, ANGLE, up), lax.ppermute(first, ANGLE, down)
    across = lax.ppermute(jnp.where(ends_plane, last, first), ANGLE, [(gap, gap + 1), (gap + 1, gap)])
    before = jnp.where(begins_plane, across, before)
    after = jnp.where(ends_plane, across, after)
    return jnp.concatenate([before, shard, after], axis=1)


def with_slab_neighbours(shard):
    up, down = shifts_of(lax.axis_size(SLAB))
    last, first = edges(shard, 0)
    return jnp.concatenate([lax.ppermute(last, SLAB, up), shard, lax.ppermute(first, SLAB, down)], axis=0)


PAD = 4
GROUP = 4
BLOCKS = ZHI * YS


def copy_rows(count):
    return count + 16 * PAD


def window_rows(bands, count):
    return bands * 2 * copy_rows(count) + count


def band_windows(offset, used, sign, band, bands, count):
    base = band * 2 * copy_rows(count)

    def start(tile):
        return base + tile * 8 + (tile & 1) * (copy_rows(count) - 8)

    first = PAD + sign * (offset - 1)
    second = jnp.where(used > 1, start(first + sign), bands * 2 * copy_rows(count))
    return pl.multiple_of(start(first), 16), pl.multiple_of(second, 16)


def fill_windows(ref, band, wide):
    count, lanes = wide.shape
    rows = copy_rows(count)
    zero = lambda n: jnp.zeros((n, lanes), wide.dtype)
    base = band * 2 * rows
    ref[base : base + rows] = jnp.concatenate([zero(8 * PAD), wide, zero(8 * PAD)], 0).astype(ref.dtype)
    ref[base + rows : base + 2 * rows] = jnp.concatenate(
        [zero(8 * (PAD - 1)), wide, zero(8 * (PAD + 1))], 0
    ).astype(ref.dtype)


def fill_zeros(ref, bands, count):
    base = bands * 2 * copy_rows(count)
    ref[base : base + count] = jnp.zeros((count, ref.shape[1]), ref.dtype)


def angle_of(j, core):
    return ((j % ZHI) * YS + j // ZHI) * CORES + core


def project_one(j, core, first_row, offsets, counts, windows, tiles, out):
    rows = tiles.shape[2]
    count, lanes = out.shape[2:]
    angle = angle_of(j, core)
    pieces = []
    for r in range(rows):
        row = first_row + r
        for start in band_windows(offsets[angle, row], counts[angle, row], 1, r, rows, count):
            pieces.append(windows[pl.ds(start, count), :])
    weights = tiles[j % ZHI, j // ZHI].reshape(len(pieces) * lanes, lanes)
    view = jnp.dot(jnp.concatenate(pieces, 1), weights, preferred_element_type=jnp.float32)
    out[j // ZHI, j % ZHI] = view


def load_project_kernel(
    place, offsets_hbm, counts_hbm, volume_hbm, tiles_hbm, out, later, windows, offsets, counts, volume, tiles, sems, more_sems
):
    core, first_row = place[0], place[1]
    rows = tiles.shape[2]
    count, lanes = out.shape[2:]
    small = [
        pltpu.make_async_copy(source, target, more_sems.at[i])
        for i, (source, target) in enumerate(
            ((volume_hbm, volume), (offsets_hbm, offsets), (counts_hbm, counts))
        )
    ]
    now = group_copies(tiles_hbm, tiles, sems, 1 - core)
    then = tile_copy(tiles_hbm, later, more_sems.at[len(small)], core, 0, BLOCKS)
    for copy in small + now:
        copy.start()
    small[0].wait()
    for r in range(rows):
        line = volume[:, r, :].astype(jnp.float32)
        fill_windows(
            windows, r, jnp.concatenate([line[:, t * lanes : (t + 1) * lanes] for t in range(line.shape[1] // lanes)], 0)
        )
    fill_zeros(windows, rows, count)
    small[1].wait()
    small[2].wait()
    for i, first in enumerate(range(0, BLOCKS, GROUP)):
        now[i].wait()
        if i == 0:
            then.start()
        for j in range(first, first + GROUP):
            project_one(j, 1 - core, first_row, offsets, counts, windows, tiles, out)
    then.wait()


def project_kernel(place, offsets, counts, windows, tiles, out):
    for j in range(ZHI * YS):
        project_one(j, place[0], place[1], offsets, counts, windows, tiles, out)


def tile_copy(tiles_hbm, tiles, sem, core, first, end):
    by_core = tiles_hbm.reshape((ZHI, YS, CORES) + tuple(tiles_hbm.shape[1:]))
    ys = pl.ds(first // ZHI, (end - first) // ZHI)
    return pltpu.make_async_copy(by_core.at[:, ys, core], tiles.at[:, ys], sem)


def group_copies(tiles_hbm, tiles, sems, core):
    return [
        tile_copy(tiles_hbm, tiles, sems.at[i], core, first, first + GROUP)
        for i, first in enumerate(range(0, BLOCKS, GROUP))
    ]


def tiles_of(tiles):
    return (ZHI, YS) + tuple(tiles.shape[1:])


def spread_group(first, core, first_row, offsets, counts, windows, tiles, begin, out):
    blocks, rows = BLOCKS, tiles.shape[2]
    count = out.shape[1]
    for r in range(rows):
        row = first_row + r
        lhs, rhs = [], []
        for j in range(first, first + GROUP):
            angle = angle_of(j, core)
            starts = band_windows(offsets[angle, row], counts[angle, row], -1, j, blocks, count)
            for k, start in enumerate(starts):
                lhs.append(windows[pl.ds(start, count), :])
                rhs.append(tiles[j % ZHI, j // ZHI, r, k])
        part = lax.dot_general(
            jnp.concatenate(lhs, 1),
            jnp.concatenate(rhs, 1),
            (((1,), (1,)), ((), ())),
            preferred_element_type=jnp.float32,
        )
        if first > 0:
            out[r] += part
        elif begin is None:
            out[r] = part
        else:
            out[r] = begin[r] + part


def fill_views(windows, views):
    blocks = ZHI * YS
    for j in range(blocks):
        fill_windows(windows, j, views[j // ZHI, j % ZHI].astype(jnp.float32))
    fill_zeros(windows, blocks, views.shape[2])


def next_x(block):
    width = block.shape[1]
    lane = lax.broadcasted_iota(jnp.int32, block.shape, 1)
    return jnp.where(lane == width - 1, 0.0, pltpu.roll(block, width - 1, 1))


def smooth(field, row):
    wide = lambda i, j: field[i, j].astype(jnp.float32)

    def flow(i, j):
        base = wide(i, j)
        steps = (wide(i + 1, j) - base, wide(i, j + 1) - base, next_x(base) - base)
        inverse = lax.rsqrt(sum(step * step for step in steps) + smooth_floor)
        return [step * inverse for step in steps]

    here = wide(1, row + 1)
    flow_z, flow_y, flow_x = flow(1, row + 1)
    lane = lax.broadcasted_iota(jnp.int32, here.shape, 1)
    edge = here * lax.rsqrt(here * here + smooth_floor)
    before_x = jnp.where(lane == 0, edge, pltpu.roll(flow_x, 1, 1))
    div = flow_z - flow(0, row + 1)[0] + flow_y - flow(1, row)[1] + flow_x - before_x
    return here + step_size * smooth_weight * div


def load_spread_kernel(place, offsets, counts, views, field, tiles_hbm, out, later, base, windows, tiles, sems, later_sem):
    now = group_copies(tiles_hbm, tiles, sems, place[0])
    then = tile_copy(tiles_hbm, later, later_sem, 1 - place[0], 0, BLOCKS)
    for copy in now:
        copy.start()
    fill_views(windows, views)
    depth, lanes = field.shape[2], base.shape[2]
    for r in range(base.shape[0]):
        line = smooth(field, r)
        for t in range(line.shape[1] // lanes):
            base[r, t * depth : (t + 1) * depth, :] = line[:, t * lanes : (t + 1) * lanes]
    for i, first in enumerate(range(0, BLOCKS, GROUP)):
        now[i].wait()
        if i == 0:
            then.start()
        spread_group(first, place[0], place[1], offsets, counts, windows, tiles, None, out)
    then.wait()


def spread_kernel(place, offsets, counts, views, tiles, begin, base, out, total, windows):
    fill_views(windows, views)
    for first in range(0, ZHI * YS, GROUP):
        spread_group(first, 1 - place[0], place[1], offsets, counts, windows, tiles, begin, total)
    depth, rows, width = out.shape
    lanes = total.shape[2]
    for r in range(rows):
        for t in range(width // lanes):
            some = slice(t * depth, (t + 1) * depth)
            out[:, r, t * lanes : (t + 1) * lanes] = base[r, some, :] - step_size * total[r, some, :]


ANY = pl.BlockSpec(memory_space=pl.ANY)
VMEM = pl.BlockSpec(memory_space=pltpu.VMEM)
SMEM = pl.BlockSpec(memory_space=pltpu.SMEM)


def params():
    return pltpu.CompilerParams(vmem_limit_bytes=16 << 20)


def cost(tiles, share):
    return pl.CostEstimate(
        flops=256 * tiles.size // share, bytes_accessed=2 * tiles.size // share, transcendentals=0
    )


def in_hbm(array):
    return pltpu.with_memory_space_constraint(array, pltpu.HBM)


def load_project(place, offsets, counts, volume, tiles):
    depth, rows, width = volume.shape
    lanes = tiles.shape[-1]
    count = depth * width // lanes
    return pl.pallas_call(
        load_project_kernel,
        in_specs=[SMEM, ANY, ANY, ANY, ANY],
        out_specs=[VMEM, VMEM, VMEM, SMEM, SMEM],
        out_shape=[
            pltpu.VMEM((YS, ZHI, count, lanes), jnp.float32),
            pltpu.VMEM(tiles_of(tiles), tiles.dtype),
            pltpu.VMEM((window_rows(rows, count), lanes), volume.dtype),
            pltpu.SMEM(offsets.shape, offsets.dtype),
            pltpu.SMEM(counts.shape, counts.dtype),
        ],
        scratch_shapes=[
            pltpu.VMEM(volume.shape, volume.dtype),
            pltpu.VMEM(tiles_of(tiles), tiles.dtype),
            pltpu.SemaphoreType.DMA((BLOCKS // GROUP,)),
            pltpu.SemaphoreType.DMA((4,)),
        ],
        compiler_params=params(),
        cost_estimate=cost(tiles, 2),
        name="load_project",
    )(place, in_hbm(offsets), in_hbm(counts), in_hbm(volume), in_hbm(tiles))


def project(place, offsets, counts, windows, tiles, like):
    return pl.pallas_call(
        project_kernel,
        in_specs=[SMEM, SMEM, SMEM, VMEM, VMEM],
        out_specs=VMEM,
        out_shape=pltpu.VMEM(like.shape, jnp.float32),
        compiler_params=params(),
        cost_estimate=cost(tiles, 2),
        name="project",
    )(place, offsets, counts, windows, tiles)


def load_spread(place, offsets, counts, views, field, tiles):
    count, lanes = views.shape[2:]
    lines = (tiles.shape[1], count, lanes)
    return pl.pallas_call(
        load_spread_kernel,
        in_specs=[SMEM, SMEM, SMEM, VMEM, VMEM, ANY],
        out_specs=[VMEM, VMEM, VMEM],
        out_shape=[
            pltpu.VMEM(lines, jnp.float32),
            pltpu.VMEM(tiles_of(tiles), tiles.dtype),
            pltpu.VMEM(lines, jnp.float32),
        ],
        scratch_shapes=[
            pltpu.VMEM((window_rows(ZHI * YS, count), lanes), jnp.bfloat16),
            pltpu.VMEM(tiles_of(tiles), tiles.dtype),
            pltpu.SemaphoreType.DMA((BLOCKS // GROUP,)),
            pltpu.SemaphoreType.DMA,
        ],
        compiler_params=params(),
        cost_estimate=cost(tiles, 2),
        name="load_spread",
    )(place, offsets, counts, views, field, in_hbm(tiles))


def spread(place, offsets, counts, views, tiles, begin, base, shape):
    count, lanes = views.shape[2:]
    return pl.pallas_call(
        spread_kernel,
        in_specs=[SMEM, SMEM, SMEM] + [VMEM] * 4,
        out_specs=VMEM,
        out_shape=jax.ShapeDtypeStruct(shape, base.dtype),
        scratch_shapes=[
            pltpu.VMEM(begin.shape, begin.dtype),
            pltpu.VMEM((window_rows(ZHI * YS, count), lanes), jnp.bfloat16),
        ],
        compiler_params=params(),
        cost_estimate=cost(tiles, 2),
        name="spread",
    )(place, offsets, counts, views, tiles, begin, base)


def own_view_kernel(place, both, out):
    depth, lanes = out.shape[1], both.shape[2]
    for t in range(out.shape[2] // lanes):
        out[0, :, t * lanes : (t + 1) * lanes] = both[place[2], t * depth : (t + 1) * depth, :]


def own_view(place, both, like):
    return pl.pallas_call(
        own_view_kernel,
        in_specs=[SMEM, VMEM],
        out_specs=VMEM,
        out_shape=jax.ShapeDtypeStruct(like.shape, like.dtype),
        compiler_params=params(),
        cost_estimate=pl.CostEstimate(flops=0, bytes_accessed=8 * like.size, transcendentals=0),
        name="own_view",
    )(place, both)


def swap(array, axis):
    return lax.ppermute(array, axis, [(0, 1), (1, 0)])


def per_device(volume, measured, ray_tiles, tile_offsets, band_counts):
    f32, bf16 = jnp.float32, jnp.bfloat16
    depth, row_count, width = volume.shape
    tile = ray_tiles.shape[3]
    tile_count = width // tile
    count = tile_count * depth
    zhi, core = lax.axis_index("zhi"), lax.axis_index("core")
    me = lax.axis_index(ANGLE)
    first_row = me * row_count
    gap = lax.axis_size(ANGLE) // ZHI - 1
    is_mine = lax.broadcasted_iota(jnp.int32, (ZHI, 1, 1), 0) == zhi
    place, is_mine, ends_plane, begins_plane = lax.optimization_barrier(
        (jnp.stack([core, first_row, zhi]), is_mine, me == gap, me == gap + 1)
    )

    away, tiles, windows, offsets, counts = load_project(
        place, tile_offsets, band_counts, volume, ray_tiles
    )
    arrived = swap(away, "core")
    kept = project(place, offsets, counts, windows, tiles, away)
    pair = kept + arrived
    pair, late_volume = lax.optimization_barrier((pair, volume))
    parts = lax.all_to_all(pair, "y", 0, 0, tiled=True)
    with_rows = with_row_neighbours(late_volume, ends_plane, begins_plane)
    parts, with_rows = lax.optimization_barrier((parts, with_rows))
    plane = jnp.sum(parts, axis=0)
    seen = measured.reshape(depth, tile_count, tile).transpose(1, 0, 2).reshape(count, tile)
    plane = plane - jnp.where(is_mine, seen[None], 0.0)
    far = swap(plane, "zhi")
    both = plane + far
    residual = own_view(place, both, measured)
    copies = jnp.broadcast_to(both.astype(bf16)[None], (YS,) + both.shape)
    views = lax.all_to_all(copies, "y", 0, 0, tiled=True)
    beside = with_slab_neighbours(with_rows)
    field = jnp.stack([lax.slice_in_dim(beside, i, i + depth, axis=0) for i in range(3)])
    field = field.transpose(0, 2, 1, 3)
    views, residual, field = lax.optimization_barrier((views, residual, field))
    views_other = swap(views, "core")
    gradient, tiles, base = load_spread(place, offsets, counts, views, field, ray_tiles)
    updated = spread(place, offsets, counts, views_other, tiles, gradient, base, volume.shape)
    return (updated, residual)


def solution(mesh):
    slabs = mesh.shape["slab"]
    fine = Mesh(
        mesh.devices.reshape(slabs // 4, 4, ZHI, YS, CORES), SLAB + ANGLE
    )
    return jax.shard_map(
        per_device,
        mesh=fine,
        in_specs=(
            P(SLAB, ANGLE, None),
            P(ANGLE, SLAB, None),
            P(None, ANGLE, None, None, None),
            P(),
            P(),
        ),
        out_specs=(P(SLAB, ANGLE, None), P(ANGLE, SLAB, None)),
        check_vma=False,
    )
```

```python
import jax
import jax.numpy as jnp
from jax import lax
from jax.experimental import pallas as pl
from jax.experimental.pallas import tpu as pltpu
from jax.sharding import Mesh, PartitionSpec as P

OFFMAX = 3

step_size = 0.3
smooth_weight = 0.2
smooth_floor = 0.25

ZHI, YS, CORES = 2, 8, 2
SLAB = ("zlo", "x")
ANGLE = ("zhi", "y", "core")

def shifts_of(size, gap=None):
    up = [(i, i + 1) for i in range(size - 1) if i != gap]
    return up, [(j, i) for i, j in up]


def edges(shard, dim):
    length = shard.shape[dim]
    return lax.slice_in_dim(shard, length - 1, length, axis=dim), lax.slice_in_dim(shard, 0, 1, axis=dim)


def with_row_neighbours(shard, ends_plane, begins_plane):
    size = lax.axis_size(ANGLE)
    gap = size // ZHI - 1
    up, down = shifts_of(size, gap)
    last, first = (edge[:, 0] for edge in edges(shard, 1))
    before, after = lax.ppermute(last, ANGLE, up), lax.ppermute(first, ANGLE, down)
    across = lax.ppermute(jnp.where(ends_plane, last, first), ANGLE, [(gap, gap + 1), (gap + 1, gap)])
    before = jnp.where(begins_plane, across, before)
    after = jnp.where(ends_plane, across, after)
    return jnp.concatenate([before[:, None], shard, after[:, None]], axis=1)


def with_slab_neighbours(shard):
    up, down = shifts_of(lax.axis_size(SLAB))
    last, first = edges(shard, 0)
    return jnp.concatenate([lax.ppermute(last, SLAB, up), shard, lax.ppermute(first, SLAB, down)], axis=0)


PAD = 4
GROUP = 4
BLOCKS = ZHI * YS


def copy_rows(count):
    return count + 16 * PAD


def window_rows(bands, count):
    return bands * 2 * copy_rows(count) + count


def band_windows(offset, used, sign, band, bands, count):
    base = band * 2 * copy_rows(count)

    def start(tile):
        return base + tile * 8 + (tile & 1) * (copy_rows(count) - 8)

    first = PAD + sign * (offset - 1)
    second = jnp.where(used > 1, start(first + sign), bands * 2 * copy_rows(count))
    return pl.multiple_of(start(first), 16), pl.multiple_of(second, 16)


def fill_windows(ref, band, wide):
    count, lanes = wide.shape
    rows = copy_rows(count)
    zero = lambda n: jnp.zeros((n, lanes), wide.dtype)
    base = band * 2 * rows
    ref[base : base + rows] = jnp.concatenate([zero(8 * PAD), wide, zero(8 * PAD)], 0).astype(ref.dtype)
    ref[base + rows : base + 2 * rows] = jnp.concatenate(
        [zero(8 * (PAD - 1)), wide, zero(8 * (PAD + 1))], 0
    ).astype(ref.dtype)


def fill_zeros(ref, bands, count):
    base = bands * 2 * copy_rows(count)
    ref[base : base + count] = jnp.zeros((count, ref.shape[1]), ref.dtype)


def angle_of(j, core):
    return ((j % ZHI) * YS + j // ZHI) * CORES + core


def project_one(j, core, first_row, offsets, counts, windows, tiles, out):
    rows = tiles.shape[2]
    count, lanes = out.shape[2:]
    angle = angle_of(j, core)
    pieces = []
    for r in range(rows):
        row = first_row + r
        for start in band_windows(offsets[angle, row], counts[angle, row], 1, r, rows, count):
            pieces.append(windows[pl.ds(start, count), :])
    weights = tiles[j % ZHI, j // ZHI].reshape(len(pieces) * lanes, lanes)
    view = jnp.dot(jnp.concatenate(pieces, 1), weights, preferred_element_type=jnp.float32)
    out[j // ZHI, j % ZHI] = view


def load_project_kernel(
    place, offsets_hbm, counts_hbm, volume_hbm, tiles_hbm, out, later, windows, offsets, counts, volume, tiles, sems, more_sems
):
    core, first_row = place[0], place[1]
    rows = tiles.shape[2]
    count, lanes = out.shape[2:]
    small = [
        pltpu.make_async_copy(source, target, more_sems.at[i])
        for i, (source, target) in enumerate(
            ((volume_hbm, volume), (offsets_hbm, offsets), (counts_hbm, counts))
        )
    ]
    now = group_copies(tiles_hbm, tiles, sems, 1 - core)
    then = tile_copy(tiles_hbm, later, more_sems.at[len(small)], core, 0, BLOCKS)
    for copy in small + now:
        copy.start()
    small[0].wait()
    for r in range(rows):
        line = volume[:, r, :].astype(jnp.float32)
        fill_windows(
            windows, r, jnp.concatenate([line[:, t * lanes : (t + 1) * lanes] for t in range(line.shape[1] // lanes)], 0)
        )
    fill_zeros(windows, rows, count)
    small[1].wait()
    small[2].wait()
    for i, first in enumerate(range(0, BLOCKS, GROUP)):
        now[i].wait()
        if i == 0:
            then.start()
        for j in range(first, first + GROUP):
            project_one(j, 1 - core, first_row, offsets, counts, windows, tiles, out)
    then.wait()


def project_kernel(place, offsets, counts, windows, tiles, out):
    for j in range(ZHI * YS):
        project_one(j, place[0], place[1], offsets, counts, windows, tiles, out)


def tile_copy(tiles_hbm, tiles, sem, core, first, end):
    by_core = tiles_hbm.reshape((ZHI, YS, CORES) + tuple(tiles_hbm.shape[1:]))
    ys = pl.ds(first // ZHI, (end - first) // ZHI)
    return pltpu.make_async_copy(by_core.at[:, ys, core], tiles.at[:, ys], sem)


def group_copies(tiles_hbm, tiles, sems, core):
    return [
        tile_copy(tiles_hbm, tiles, sems.at[i], core, first, first + GROUP)
        for i, first in enumerate(range(0, BLOCKS, GROUP))
    ]


def tiles_of(tiles):
    return (ZHI, YS) + tuple(tiles.shape[1:])


def spread_group(first, core, first_row, offsets, counts, windows, tiles, begin, out):
    blocks, rows = BLOCKS, tiles.shape[2]
    count = out.shape[1]
    for r in range(rows):
        row = first_row + r
        lhs, rhs = [], []
        for j in range(first, first + GROUP):
            angle = angle_of(j, core)
            starts = band_windows(offsets[angle, row], counts[angle, row], -1, j, blocks, count)
            for k, start in enumerate(starts):
                lhs.append(windows[pl.ds(start, count), :])
                rhs.append(tiles[j % ZHI, j // ZHI, r, k])
        part = lax.dot_general(
            jnp.concatenate(lhs, 1),
            jnp.concatenate(rhs, 1),
            (((1,), (1,)), ((), ())),
            preferred_element_type=jnp.float32,
        )
        if first > 0:
            out[r] += part
        elif begin is None:
            out[r] = part
        else:
            out[r] = begin[r] + part


def fill_views(windows, views):
    blocks = ZHI * YS
    for j in range(blocks):
        fill_windows(windows, j, views[j // ZHI, j % ZHI].astype(jnp.float32))
    fill_zeros(windows, blocks, views.shape[2])


def next_x(block):
    width = block.shape[1]
    lane = lax.broadcasted_iota(jnp.int32, block.shape, 1)
    return jnp.where(lane == width - 1, 0.0, pltpu.roll(block, width - 1, 1))


def smooth(field, row):
    wide = lambda i, j: field[i, j].astype(jnp.float32)

    def flow(i, j):
        base = wide(i, j)
        steps = (wide(i + 1, j) - base, wide(i, j + 1) - base, next_x(base) - base)
        inverse = lax.rsqrt(sum(step * step for step in steps) + smooth_floor)
        return [step * inverse for step in steps]

    here = wide(1, row + 1)
    flow_z, flow_y, flow_x = flow(1, row + 1)
    lane = lax.broadcasted_iota(jnp.int32, here.shape, 1)
    edge = here * lax.rsqrt(here * here + smooth_floor)
    before_x = jnp.where(lane == 0, edge, pltpu.roll(flow_x, 1, 1))
    div = flow_z - flow(0, row + 1)[0] + flow_y - flow(1, row)[1] + flow_x - before_x
    return here + step_size * smooth_weight * div


def load_spread_kernel(place, offsets, counts, views, field, tiles_hbm, out, later, base, windows, tiles, sems, later_sem):
    now = group_copies(tiles_hbm, tiles, sems, place[0])
    then = tile_copy(tiles_hbm, later, later_sem, 1 - place[0], 0, BLOCKS)
    for copy in now:
        copy.start()
    fill_views(windows, views)
    depth, lanes = field.shape[2], base.shape[2]
    for r in range(base.shape[0]):
        line = smooth(field, r)
        for t in range(line.shape[1] // lanes):
            base[r, t * depth : (t + 1) * depth, :] = line[:, t * lanes : (t + 1) * lanes]
    for i, first in enumerate(range(0, BLOCKS, GROUP)):
        now[i].wait()
        if i == 0:
            then.start()
        spread_group(first, place[0], place[1], offsets, counts, windows, tiles, None, out)
    then.wait()


def spread_kernel(place, offsets, counts, views, tiles, begin, base, out, total, windows):
    fill_views(windows, views)
    for first in range(0, ZHI * YS, GROUP):
        spread_group(first, 1 - place[0], place[1], offsets, counts, windows, tiles, begin, total)
    depth, rows, width = out.shape
    lanes = total.shape[2]
    for r in range(rows):
        for t in range(width // lanes):
            some = slice(t * depth, (t + 1) * depth)
            out[:, r, t * lanes : (t + 1) * lanes] = base[r, some, :] - step_size * total[r, some, :]


ANY = pl.BlockSpec(memory_space=pl.ANY)
VMEM = pl.BlockSpec(memory_space=pltpu.VMEM)
SMEM = pl.BlockSpec(memory_space=pltpu.SMEM)


def params():
    return pltpu.CompilerParams(vmem_limit_bytes=16 << 20)


def cost(tiles, share):
    return pl.CostEstimate(
        flops=256 * tiles.size // share, bytes_accessed=2 * tiles.size // share, transcendentals=0
    )


def in_hbm(array):
    return pltpu.with_memory_space_constraint(array, pltpu.HBM)


def load_project(place, offsets, counts, volume, tiles):
    depth, rows, width = volume.shape
    lanes = tiles.shape[-1]
    count = depth * width // lanes
    return pl.pallas_call(
        load_project_kernel,
        in_specs=[SMEM, ANY, ANY, ANY, ANY],
        out_specs=[VMEM, VMEM, VMEM, SMEM, SMEM],
        out_shape=[
            pltpu.VMEM((YS, ZHI, count, lanes), jnp.float32),
            pltpu.VMEM(tiles_of(tiles), tiles.dtype),
            pltpu.VMEM((window_rows(rows, count), lanes), volume.dtype),
            pltpu.SMEM(offsets.shape, offsets.dtype),
            pltpu.SMEM(counts.shape, counts.dtype),
        ],
        scratch_shapes=[
            pltpu.VMEM(volume.shape, volume.dtype),
            pltpu.VMEM(tiles_of(tiles), tiles.dtype),
            pltpu.SemaphoreType.DMA((BLOCKS // GROUP,)),
            pltpu.SemaphoreType.DMA((4,)),
        ],
        compiler_params=params(),
        cost_estimate=cost(tiles, 2),
        name="load_project",
    )(place, in_hbm(offsets), in_hbm(counts), in_hbm(volume), in_hbm(tiles))


def project(place, offsets, counts, windows, tiles, like):
    return pl.pallas_call(
        project_kernel,
        in_specs=[SMEM, SMEM, SMEM, VMEM, VMEM],
        out_specs=VMEM,
        out_shape=pltpu.VMEM(like.shape, jnp.float32),
        compiler_params=params(),
        cost_estimate=cost(tiles, 2),
        name="project",
    )(place, offsets, counts, windows, tiles)


def load_spread(place, offsets, counts, views, field, tiles):
    count, lanes = views.shape[2:]
    lines = (tiles.shape[1], count, lanes)
    return pl.pallas_call(
        load_spread_kernel,
        in_specs=[SMEM, SMEM, SMEM, VMEM, VMEM, ANY],
        out_specs=[VMEM, VMEM, VMEM],
        out_shape=[
            pltpu.VMEM(lines, jnp.float32),
            pltpu.VMEM(tiles_of(tiles), tiles.dtype),
            pltpu.VMEM(lines, jnp.float32),
        ],
        scratch_shapes=[
            pltpu.VMEM((window_rows(ZHI * YS, count), lanes), jnp.bfloat16),
            pltpu.VMEM(tiles_of(tiles), tiles.dtype),
            pltpu.SemaphoreType.DMA((BLOCKS // GROUP,)),
            pltpu.SemaphoreType.DMA,
        ],
        compiler_params=params(),
        cost_estimate=cost(tiles, 2),
        name="load_spread",
    )(place, offsets, counts, views, field, in_hbm(tiles))


def spread(place, offsets, counts, views, tiles, begin, base, shape):
    count, lanes = views.shape[2:]
    return pl.pallas_call(
        spread_kernel,
        in_specs=[SMEM, SMEM, SMEM] + [VMEM] * 4,
        out_specs=VMEM,
        out_shape=jax.ShapeDtypeStruct(shape, base.dtype),
        scratch_shapes=[
            pltpu.VMEM(begin.shape, begin.dtype),
            pltpu.VMEM((window_rows(ZHI * YS, count), lanes), jnp.bfloat16),
        ],
        compiler_params=params(),
        cost_estimate=cost(tiles, 2),
        name="spread",
    )(place, offsets, counts, views, tiles, begin, base)


def own_view_kernel(place, both, out):
    depth, lanes = out.shape[1], both.shape[2]
    for t in range(out.shape[2] // lanes):
        out[0, :, t * lanes : (t + 1) * lanes] = both[place[2], t * depth : (t + 1) * depth, :]


def own_view(place, both, like):
    return pl.pallas_call(
        own_view_kernel,
        in_specs=[SMEM, VMEM],
        out_specs=VMEM,
        out_shape=jax.ShapeDtypeStruct(like.shape, like.dtype),
        compiler_params=params(),
        cost_estimate=pl.CostEstimate(flops=0, bytes_accessed=8 * like.size, transcendentals=0),
        name="own_view",
    )(place, both)


def swap(array, axis):
    return lax.ppermute(array, axis, [(0, 1), (1, 0)])


def per_device(volume, measured, ray_tiles, tile_offsets, band_counts):
    f32, bf16 = jnp.float32, jnp.bfloat16
    depth, row_count, width = volume.shape
    tile = ray_tiles.shape[3]
    tile_count = width // tile
    count = tile_count * depth
    zhi, core = lax.axis_index("zhi"), lax.axis_index("core")
    me = lax.axis_index(ANGLE)
    first_row = me * row_count
    gap = lax.axis_size(ANGLE) // ZHI - 1
    is_mine = lax.broadcasted_iota(jnp.int32, (ZHI, 1, 1), 0) == zhi
    place, is_mine, ends_plane, begins_plane = lax.optimization_barrier(
        (jnp.stack([core, first_row, zhi]), is_mine, me == gap, me == gap + 1)
    )

    away, tiles, windows, offsets, counts = load_project(
        place, tile_offsets, band_counts, volume, ray_tiles
    )
    arrived = swap(away, "core")
    kept = project(place, offsets, counts, windows, tiles, away)
    pair = kept + arrived
    pair, late_volume = lax.optimization_barrier((pair, volume))
    parts = lax.all_to_all(pair, "y", 0, 0, tiled=True)
    with_rows = with_row_neighbours(late_volume, ends_plane, begins_plane)
    parts, with_rows = lax.optimization_barrier((parts, with_rows))
    plane = jnp.sum(parts, axis=0)
    seen = measured.reshape(depth, tile_count, tile).transpose(1, 0, 2).reshape(count, tile)
    plane = plane - jnp.where(is_mine, seen[None], 0.0)
    far = swap(plane, "zhi")
    both = plane + far
    residual = own_view(place, both, measured)
    copies = jnp.broadcast_to(both.astype(bf16)[None], (YS,) + both.shape)
    views = lax.all_to_all(copies, "y", 0, 0, tiled=True)
    beside = with_slab_neighbours(with_rows)
    field = jnp.stack([lax.slice_in_dim(beside, i, i + depth, axis=0) for i in range(3)])
    field = field.transpose(0, 2, 1, 3)
    views, residual, field = lax.optimization_barrier((views, residual, field))
    views_other = swap(views, "core")
    gradient, tiles, base = load_spread(place, offsets, counts, views, field, ray_tiles)
    updated = spread(place, offsets, counts, views_other, tiles, gradient, base, volume.shape)
    return (updated, residual)


def solution(mesh):
    slabs = mesh.shape["slab"]
    fine = Mesh(
        mesh.devices.reshape(slabs // 4, 4, ZHI, YS, CORES), SLAB + ANGLE
    )
    return jax.shard_map(
        per_device,
        mesh=fine,
        in_specs=(
            P(SLAB, ANGLE, None),
            P(ANGLE, SLAB, None),
            P(None, ANGLE, None, None, None),
            P(),
            P(),
        ),
        out_specs=(P(SLAB, ANGLE, None), P(ANGLE, SLAB, None)),
        check_vma=False,
    )
```
